512 devices in a mesh: query: 32 (over z, core), passage: 16 (over x, y).
Axes of the slice: x: 4, y: 4, z: 16, core: 2. Of those that a mesh axis runs over, the one named last changes fastest.
Arguments:
- queries: bfloat16 [2048, 32, 128], P(('query', 'passage')), may hold values from -60 to 60
- hidden: bfloat16 [2048, 180, 768], P(('query', 'passage')), may hold values from -24 to 24
- proj: bfloat16 [768, 128], replicated, may hold values from -0.21875 to 0.21875
- lists: int32 [2048, 64], P(('query', 'passage')), may hold values from 0 to 63
Outputs:
- losses: float32 [2048], P(('query', 'passage'))
- w_grad: float32 [768, 128], P('passage')
The draws below stay inside these ranges and needn't reach their ends.
Inputs may be any that keep to these rules, and one draw needn't show every extreme that they name: `lists`: queries of one row only list passages of that same row; entry 0 of each list is the query's positive passage.
All inputs are finite; a program needn't handle non-finite values.
Results may differ from the reference program's by a relative error of at most 0.0075.
The reference program's roundings to bfloat16 on the way (of `embed`, `weight` and `d_flat`) count: a program that leaves them out, or rounds other values in their place, can miss the bound.
Values may be sent and summed in bfloat16 or wider, within the bound.
A program may use at most 64 MiB of HBM per device.

```python
import math
import jax
import jax.numpy as jnp
import numpy as np
from jax import lax

D = 768
DIM = 128
QT = 32
PT = 180
NEG = 64
QROW = 64
PROW = 64
NQ = 2048
NP = 2048


def draw_queries(key, part):
    base = jax.random.normal(key, (NQ, QT, DIM), jnp.float32)
    return jnp.clip(base, -60.0, 60.0).astype(jnp.bfloat16)


def place_ends(drawn, own_key, least, high):
    spot = [jax.random.randint(jax.random.fold_in(own_key, axis), (), 0, length) for axis, length in enumerate(drawn.shape)]
    longest = drawn.shape.index(max(drawn.shape))
    next_to = spot[:longest] + [(spot[longest] + 1) % drawn.shape[longest]] + spot[longest + 1:]
    return drawn.at[tuple(spot)].set(least).at[tuple(next_to)].set(high)


def raised(entries, key, source, target, parts, factor):
    def block_of(position):
        return (jnp.arange(entries.shape[position]) // (entries.shape[position] // parts)).reshape((-1,) + (1,) * (entries.ndim - 1 - position))

    first = jax.random.permutation(key, parts)[block_of(target)]
    far = (block_of(target) + parts // 2) % parts
    return jnp.where((block_of(source) == first) | (block_of(source) == far), factor * entries, entries)


def block_scale(rng, dims, cuts, least, top_value):
    loudness = 1.0
    for axis_at, parts in cuts:
        steps = jax.random.uniform(jax.random.fold_in(jax.random.fold_in(rng, 6), axis_at), (parts,), jnp.float32, least / len(cuts), top_value / len(cuts))
        loudness = loudness * jnp.repeat(jnp.exp(steps), dims[axis_at] // parts).reshape((-1,) + (1,) * (len(dims) - 1 - axis_at))
    return loudness


def rank_bounds(number_of, lean):
    portions = [(1 << 20) // math.isqrt(rank ** lean) + 1 for rank in range(1, number_of + 1)]
    width = 1 + sum(portions) // (1 << 30)
    return np.cumsum(np.array([max(1, weight // width) for weight in portions]))


def ranked(rng, dims, amount, lean):
    table = rank_bounds(amount, lean)
    lot = jax.random.randint(jax.random.fold_in(rng, 1), dims, 0, int(table[amount - 1]))
    grade = jnp.searchsorted(jnp.asarray(table, jnp.int32), lot, side="right")
    return jax.random.permutation(jax.random.fold_in(rng, 2), amount)[grade].astype(jnp.int32)


def bell_draw(stream_key, extent, scale, bound, pieces=(), kind=jnp.bfloat16):
    values = scale * jax.random.normal(stream_key, extent, jnp.float32)
    if pieces:
        values = values * block_scale(stream_key, extent, pieces, -0.22, 0.18)
    return jnp.clip(values, -bound, bound).astype(kind)


def bell_draw_with(stream_key, dims, scale, limit, cuts, heavy, kind=jnp.bfloat16):
    drawn = scale * jax.random.normal(stream_key, dims, jnp.float32)
    if cuts:
        drawn = drawn * block_scale(stream_key, dims, cuts, -0.22, 0.18)
    return jnp.clip(raised(drawn, jax.random.fold_in(stream_key, 3), *heavy), -limit, limit).astype(kind)


def setup_inputs(seed: int = 0) -> dict:
    streams_of = jax.random.split(jax.random.key(seed), 5)
    return {
        "queries": draw_queries(jax.random.fold_in(streams_of[4], 71), 0),
        "hidden": bell_draw_with(streams_of[1], (NP, PT, D), 1.0, 24.0, ((0, 512),), (0, 2, 256, 6.0)),
        "proj": bell_draw(streams_of[2], (D, DIM), D ** -0.5, 0.21875),
        "lists": place_ends(ranked(streams_of[3], (NQ, NEG), PROW, 2), jax.random.fold_in(streams_of[3], 3), 0, PROW - 1).astype(jnp.int32),
    }


BETA = 4.0
EPS = 1e-06

def row_scores(qrow, erow):
    qflat = qrow.reshape(-1, DIM)

    def single(emb):
        sims = jnp.dot(emb, qflat.T, preferred_element_type=jnp.float32)
        lse = jax.nn.logsumexp(BETA * sims, axis=0)
        return lax.optimization_barrier(jnp.sum(lse.reshape(QROW, QT), axis=1)) / BETA
    return lax.map(single, erow).T

def row_grads(qrow, erow, coef):
    qflat = qrow.reshape(-1, DIM)

    def single(args):
        emb, column = args
        sims = jnp.dot(emb, qflat.T, preferred_element_type=jnp.float32)
        probs = jax.nn.softmax(BETA * sims, axis=0)
        weight = (probs * jnp.repeat(column, QT)[None, :]).astype(jnp.bfloat16)
        return jnp.dot(weight, qflat, preferred_element_type=jnp.float32)
    return lax.map(single, (erow, coef.T))

def reference(queries, hidden, proj, lists):
    flat = jnp.dot(hidden.reshape(-1, D), proj, preferred_element_type=jnp.float32)
    norm = jnp.sqrt(lax.optimization_barrier(jnp.sum(flat * flat, axis=1, keepdims=True)) + EPS)
    unit = flat / norm
    embed = unit.astype(jnp.bfloat16).reshape(NP // PROW, PROW, PT, DIM)
    qrows = queries.reshape(NQ // QROW, QROW, QT, DIM)
    lrows = lists.reshape(NQ // QROW, QROW, NEG)
    columns = jnp.arange(PROW, dtype=jnp.int32)
    target = (jnp.arange(NEG, dtype=jnp.int32) == 0).astype(jnp.float32)

    def per_row(args):
        qrow, erow, lrow = args
        scores = row_scores(qrow, erow)
        onehot = (lrow[:, :, None] == columns[None, None, :]).astype(jnp.float32)
        listed = jnp.einsum('qkp,qp->qk', onehot, scores, precision=lax.Precision.HIGHEST)
        loss = jax.nn.logsumexp(listed, axis=1) - listed[:, 0]
        probs = jax.nn.softmax(listed, axis=1)
        coef = jnp.einsum('qkp,qk->qp', onehot, probs - target[None, :], precision=lax.Precision.HIGHEST) / NQ
        return (loss, row_grads(qrow, erow, coef))
    losses, grads = lax.map(per_row, (qrows, embed, lrows))
    d_embed = grads.reshape(-1, DIM)
    d_flat = ((d_embed - unit * lax.optimization_barrier(jnp.sum(d_embed * unit, axis=1, keepdims=True))) / norm).astype(jnp.bfloat16)
    w_grad = jnp.dot(hidden.reshape(-1, D).T, d_flat, preferred_element_type=jnp.float32)
    return (losses.reshape(NQ), w_grad)
```

```python
import functools

import jax
import jax.numpy as jnp
from jax import lax
from jax.experimental import pallas as pl
from jax.experimental.pallas import tpu as pltpu
from jax.sharding import PartitionSpec as P

BETA = 4.0
EPS = 1e-06
SIDE = 4
ROWS = SIDE * SIDE
F32 = jnp.float32
BF16 = jnp.bfloat16
NEGBIG = -3.0e38
MESH = pl.DeviceIdType.MESH


def gray(index):
    return index ^ (index >> 1)


def spread(tile, lane, block):
    own = jnp.where(lane // 8 == block, tile, 0.0)
    for step in (8, 16, 32, 64):
        own = own + pltpu.roll(own, step, 1)
    return own


def kernel(
    total,
    queries_ref, hidden_ref, proj_ref, lists_ref,
    loss_ref, grad_ref,
    qbuf, meta, mrows, mcols, embed, unit, norm, expo, rsum, score, scale,
    part, precv, rsend, rrecv, zbuf, fin,
    qs, qr, ms, mr, ss, sr, ps, rs, rr, zs, zr, fs,
):
    qcount, qtok, width = queries_ref.shape
    pcount, ptok, hwidth = hidden_ref.shape
    nz = lax.axis_size("query") // 2
    qid = lax.axis_index("query")
    me = lax.axis_index("passage")
    mx, my = me // SIDE, me % SIDE
    mz, core = qid // 2, qid % 2
    partner = {"query": mz * 2 + (1 - core)}
    block = qcount * qtok
    half = grad_ref.shape[0] // 2

    def peer_of(slot):
        dx, dy = gray(slot // SIDE), gray(slot % SIDE)
        return ((mx + dx) % SIDE) * SIDE + (my + dy) % SIDE

    def back_of(slot):
        dx, dy = gray(slot // SIDE), gray(slot % SIDE)
        return ((mx + SIDE - dx) % SIDE) * SIDE + (my + SIDE - dy) % SIDE

    barrier = pltpu.get_barrier_semaphore()
    for slot in range(1, ROWS):
        pl.semaphore_signal(barrier, inc=1, device_id={"passage": peer_of(slot)}, device_id_type=MESH)

    def greet(step, carry):
        zpeer = (mz + step) % nz
        pl.semaphore_signal(barrier, inc=1, device_id={"query": zpeer * 2 + core}, device_id_type=MESH)
        return carry

    lax.fori_loop(1, nz, greet, 0)
    pl.semaphore_signal(barrier, inc=1, device_id=partner, device_id_type=MESH)

    lane = lax.broadcasted_iota(jnp.int32, (8, 128), 1)
    row = lax.broadcasted_iota(jnp.int32, (block, block), 0)
    col = lax.broadcasted_iota(jnp.int32, (block, block), 1)
    order = jnp.where(col == (row % qcount) * qtok + row // qcount, 1.0, 0.0).astype(BF16)
    mine = jnp.dot(order, queries_ref[...].reshape(block, width), preferred_element_type=F32)
    qbuf[0:block, :] = mine.astype(BF16)

    listed = jnp.concatenate(
        [lists_ref[...].astype(F32), jnp.zeros((qcount, 128 - lists_ref.shape[1]), F32)], axis=1
    )
    listed = jnp.concatenate([listed, jnp.zeros((128 - qcount, 128), F32)], axis=0).T
    listed = listed[: lists_ref.shape[1], :]
    lrow = lax.broadcasted_iota(jnp.int32, (lists_ref.shape[1], 128), 1)
    number = jnp.where(lrow % 8 < pcount, (lrow // 8) * pcount + lrow % 8, -1).astype(F32)
    counts, firsts = [], []
    for query in range(qcount):
        hit = jnp.where(listed[:, query : query + 1] == number, 1.0, 0.0)
        counts.append(jnp.sum(hit, axis=0, keepdims=True))
        firsts.append(hit[0:1, :])
    tile = jnp.concatenate(counts + firsts, axis=0)
    meta[0] = jnp.concatenate([tile, jnp.zeros_like(tile)], axis=0).astype(BF16)

    pl.semaphore_wait(barrier, ROWS - 1 + nz - 1 + 1)

    def query_copy(slot):
        return pltpu.make_async_remote_copy(
            src_ref=qbuf.at[pl.ds(0, block)],
            dst_ref=qbuf.at[pl.ds(slot * block, block)],
            send_sem=qs.at[slot], recv_sem=qr.at[slot],
            device_id={"passage": back_of(slot)}, device_id_type=MESH,
        )

    def meta_copy(slot):
        return pltpu.make_async_remote_copy(
            src_ref=meta.at[0], dst_ref=meta.at[slot],
            send_sem=ms.at[slot], recv_sem=mr.at[slot],
            device_id={"passage": back_of(slot)}, device_id_type=MESH,
        )

    def score_copy(slot):
        return pltpu.make_async_remote_copy(
            src_ref=score.at[0], dst_ref=score.at[slot],
            send_sem=ss.at[slot], recv_sem=sr.at[slot],
            device_id={"passage": back_of(slot)}, device_id_type=MESH,
        )

    for slot in range(1, ROWS):
        query_copy(slot).start()
    for slot in range(1, ROWS):
        meta_copy(slot).start()

    def project(passage, carry):
        flat = jnp.dot(hidden_ref[passage], proj_ref[...], preferred_element_type=F32)
        size = jnp.sqrt(jnp.sum(flat * flat, axis=1, keepdims=True) + EPS)
        one = flat / size
        norm[passage] = jnp.broadcast_to(size, one.shape)
        unit[passage] = one
        embed[passage] = one.astype(BF16)
        return carry

    lax.fori_loop(0, pcount, project, 0)

    def score_pair(pair, found):
        @pl.when(pair > 0)
        def _():
            query_copy(2 * pair).wait_recv()

        query_copy(2 * pair + 1).wait_recv()
        start = pl.multiple_of(pair * 2 * block, 2 * block)
        both = qbuf[pl.ds(start, 2 * block), :]
        lses = []
        for passage in range(pcount):
            sims = lax.dot_general(
                embed[passage], both, (((1,), (1,)), ((), ())), preferred_element_type=F32
            )
            top = jnp.max(sims, axis=0, keepdims=True)
            raised = jnp.exp(BETA * (sims - top))
            expo[pair, passage] = raised
            total_e = jnp.sum(raised, axis=0, keepdims=True)
            rsum[pair, passage : passage + 1] = 1.0 / total_e
            lses.append(jnp.log(total_e) + BETA * top)
        lse = jnp.concatenate(lses + lses, axis=0)
        for which in range(2):
            summed = lse[:, which * block : (which + 1) * block]
            for step in (4, 8, 16, 32, 64):
                summed = summed + pltpu.roll(summed, step, 1)
            found = jnp.where(lane // 8 == peer_of(2 * pair + which), summed, found)
        return found

    found = lax.fori_loop(0, ROWS // 2, score_pair, jnp.zeros((8, 128), F32))
    score[0] = found / BETA

    for slot in range(1, ROWS):
        score_copy(slot).start()

    for slot in range(ROWS):
        if slot:
            meta_copy(slot).wait_recv()
        mrows[pl.ds(pl.multiple_of(8 * peer_of(slot), 8), 8), :] = meta[slot].astype(F32)[0:8]
    mcols[...] = mrows[...].T

    top = jnp.full((8, 128), NEGBIG, F32)
    for slot in range(ROWS):
        if slot:
            score_copy(slot).wait_recv()
        count = mcols[pl.ds(pl.multiple_of(8 * peer_of(slot), 8), 8), :]
        top = jnp.maximum(top, jnp.where(count > 0, score[slot], NEGBIG))
    top = jnp.max(top, axis=0, keepdims=True)
    mass = jnp.zeros((8, 128), F32)
    shares = None
    for slot in range(ROWS):
        count = mcols[pl.ds(pl.multiple_of(8 * peer_of(slot), 8), 8), :]
        term = jnp.where(count > 0, count * jnp.exp(jnp.where(count > 0, score[slot], top) - top), 0.0)
        mass = mass + term
        if slot == 0:
            shares = term
    mass = jnp.sum(mass, axis=0, keepdims=True)
    top, mass = jnp.broadcast_to(top, (8, 128)), jnp.broadcast_to(mass, (8, 128))
    loss = jnp.log(mass) + top - pltpu.roll(top, 124, 1)
    loss = jnp.where(lane % 8 < 4, loss, pltpu.roll(loss, 4, 1))
    loss_ref[...] = spread(loss, lane, me)[0:1, :qcount]
    probs = shares / mass
    coef = (probs - pltpu.roll(probs, 124, 1)) / total
    coef = jnp.where(lane % 8 < 4, coef, pltpu.roll(coef, 4, 1))

    def make_scale(pair, carry):
        for which in range(2):
            wide = spread(coef, lane, peer_of(2 * pair + which))[0:pcount]
            scale[pair, :, which * block : (which + 1) * block] = (
                wide * rsum[pair, :, which * block : (which + 1) * block]
            )
        return carry

    lax.fori_loop(0, ROWS // 2, make_scale, 0)

    part[...] = jnp.zeros_like(part)

    def passage_grad(passage, carry):
        def pair_grad(pair, acc):
            weight = (expo[pair, passage] * scale[pair, pl.ds(passage, 1), :]).astype(BF16)
            start = pl.multiple_of(pair * 2 * block, 2 * block)
            return acc + jnp.dot(weight, qbuf[pl.ds(start, 2 * block), :], preferred_element_type=F32)

        d_embed = lax.fori_loop(0, ROWS // 2, pair_grad, jnp.zeros((ptok, width), F32))
        one = unit[passage]
        along = jnp.sum(d_embed * one, axis=1, keepdims=True)
        d_flat = ((d_embed - one * along) / norm[passage]).astype(BF16)
        grown = lax.dot_general(
            hidden_ref[passage], d_flat, (((0,), (0,)), ((), ())), preferred_element_type=F32
        )
        part[...] += grown.reshape(part.shape)
        return carry

    lax.fori_loop(0, pcount, passage_grad, 0)

    pair_copy = pltpu.make_async_remote_copy(
        src_ref=part.at[:, 1 - core], dst_ref=precv,
        send_sem=ps.at[0], recv_sem=ps.at[1], device_id=partner, device_id_type=MESH,
    )
    pair_copy.start()
    pair_copy.wait_recv()
    rsend[...] = part[:, core] + precv[...]

    def grad_copy(slot):
        return pltpu.make_async_remote_copy(
            src_ref=rsend.at[back_of(slot)], dst_ref=rrecv.at[slot],
            send_sem=rs.at[slot], recv_sem=rr.at[slot],
            device_id={"passage": back_of(slot)}, device_id_type=MESH,
        )

    for slot in range(1, ROWS):
        grad_copy(slot).start()
    acc = rsend[me]
    for slot in range(1, ROWS):
        grad_copy(slot).wait_recv()
        acc = acc + rrecv[slot]
    zbuf[mz] = acc

    def z_copy(step):
        return pltpu.make_async_remote_copy(
            src_ref=zbuf.at[mz], dst_ref=zbuf.at[mz],
            send_sem=zs.at[step], recv_sem=zr.at[step],
            device_id={"query": ((mz + step) % nz) * 2 + core}, device_id_type=MESH,
        )

    def z_arrival(step):
        source = (mz + nz - step) % nz
        return pltpu.make_async_remote_copy(
            src_ref=zbuf.at[source], dst_ref=zbuf.at[source],
            send_sem=zs.at[step], recv_sem=zr.at[step],
            device_id={"query": ((mz + step) % nz) * 2 + core}, device_id_type=MESH,
        )

    for step in range(1, nz):
        z_copy(step).start()
    for step in range(1, nz):
        z_arrival(step).wait_recv()
    acc = zbuf[0]
    for step in range(1, nz):
        acc = acc + zbuf[step]
    fin[core] = acc
    fin_copy = pltpu.make_async_remote_copy(
        src_ref=fin.at[core], dst_ref=fin.at[core],
        send_sem=fs.at[0], recv_sem=fs.at[1], device_id=partner, device_id_type=MESH,
    )
    fin_copy.start()
    for slot in range(1, ROWS):
        query_copy(slot).wait_send()
        meta_copy(slot).wait_send()
        score_copy(slot).wait_send()
        grad_copy(slot).wait_send()
    pair_copy.wait_send()
    for step in range(1, nz):
        z_copy(step).wait_send()
    fin_arrival = pltpu.make_async_remote_copy(
        src_ref=fin.at[1 - core], dst_ref=fin.at[1 - core],
        send_sem=fs.at[0], recv_sem=fs.at[1], device_id=partner, device_id_type=MESH,
    )
    fin_arrival.wait_recv()
    fin_copy.wait_send()
    grad_ref[...] = fin[...].reshape(grad_ref.shape)


def body(queries, hidden, proj, lists):
    qcount, qtok, width = queries.shape
    pcount, ptok, hwidth = hidden.shape
    nside = lax.axis_size("passage")
    nq = lax.axis_size("query")
    total = qcount * nq * nside
    share = hwidth // nside
    block = qcount * qtok
    pairs = nside // 2
    nz = nq // 2
    dma = pltpu.SemaphoreType.DMA
    losses, grad = pl.pallas_call(
        functools.partial(kernel, total),
        out_shape=(
            jax.ShapeDtypeStruct((1, qcount), F32),
            jax.ShapeDtypeStruct((share, width), F32),
        ),
        in_specs=[pl.BlockSpec(memory_space=pltpu.VMEM)] * 4,
        out_specs=(pl.BlockSpec(memory_space=pltpu.VMEM),) * 2,
        scratch_shapes=[
            pltpu.VMEM((nside * block, width), BF16),
            pltpu.VMEM((nside, 16, 128), BF16),
            pltpu.VMEM((128, 128), F32),
            pltpu.VMEM((128, 128), F32),
            pltpu.VMEM((pcount, ptok, width), BF16),
            pltpu.VMEM((pcount, ptok, width), F32),
            pltpu.VMEM((pcount, ptok, width), F32),
            pltpu.VMEM((pairs, pcount, ptok, 2 * block), F32),
            pltpu.VMEM((pairs, pcount, 2 * block), F32),
            pltpu.VMEM((nside, 8, 128), F32),
            pltpu.VMEM((pairs, pcount, 2 * block), F32),
            pltpu.VMEM((nside, 2, share // 2, width), F32),
            pltpu.VMEM((nside, share // 2, width), F32),
            pltpu.VMEM((nside, share // 2, width), F32),
            pltpu.VMEM((nside, share // 2, width), F32),
            pltpu.VMEM((nz, share // 2, width), F32),
            pltpu.VMEM((2, share // 2, width), F32),
            dma((nside,)), dma((nside,)),
            dma((nside,)), dma((nside,)),
            dma((nside,)), dma((nside,)),
            dma((2,)),
            dma((nside,)), dma((nside,)),
            dma((nz,)), dma((nz,)),
            dma((2,)),
        ],
        compiler_params=pltpu.CompilerParams(
            collective_id=0, has_side_effects=True, vmem_limit_bytes=60 * 1024 * 1024
        ),
        name="retriever_step",
    )(queries, hidden, proj, lists)
    return (losses.reshape(qcount), grad)


def solution(mesh):
    placed = (
        P(("query", "passage"), None, None),
        P(("query", "passage"), None, None),
        P(),
        P(("query", "passage"), None),
    )
    return jax.shard_map(
        body,
        mesh=mesh,
        in_specs=placed,
        out_specs=(P(("query", "passage")), P("passage", None)),
        check_vma=False,
    )
```

```python
import functools

import jax
import jax.numpy as jnp
from jax import lax
from jax.experimental import pallas as pl
from jax.experimental.pallas import tpu as pltpu
from jax.sharding import PartitionSpec as P

BETA = 4.0
EPS = 1e-06
SIDE = 4
ROWS = SIDE * SIDE
F32 = jnp.float32
BF16 = jnp.bfloat16
NEGBIG = -3.0e38
PARTS = 3
MESH = pl.DeviceIdType.MESH


def gray(index):
    return index ^ (index >> 1)


def spread(tile, lane, block):
    own = jnp.where(lane // 8 == block, tile, 0.0)
    for step in (8, 16, 32, 64):
        own = own + pltpu.roll(own, step, 1)
    return own


def kernel(
    total,
    queries_hbm, hidden_hbm, proj_hbm, lists_hbm,
    loss_ref, grad_ref,
    queries_ref, hidden_ref, proj_ref, lists_ref,
    qbuf, meta, mrows, mcols, turned, embed, unit, norm, expo, rsum, score, scale,
    part, precv, rsend, rrecv, zbuf, fin,
    ins, qs, qr, ms, mr, ss, sr, ps, rs, rr, zs, zr, fs, tok,
):
    qcount, qtok, width = queries_ref.shape
    ptok, pcount, hwidth = hidden_ref.shape
    nz = lax.axis_size("query") // 2
    qid = lax.axis_index("query")
    me = lax.axis_index("passage")
    mx, my = me // SIDE, me % SIDE
    mz, core = qid // 2, qid % 2
    partner = {"query": mz * 2 + (1 - core)}
    block = qcount * qtok
    half = grad_ref.shape[0] // 2
    piece = ptok * pcount // PARTS

    def along(step):
        return {"query": ((mz + nz + step) % nz) * 2 + core}

    loads = [
        pltpu.make_async_copy(src, dst, ins.at[n])
        for n, (src, dst) in enumerate(
            [(queries_hbm, queries_ref), (lists_hbm, lists_ref), (proj_hbm, proj_ref), (hidden_hbm, hidden_ref)]
        )
    ]

    def peer_of(slot):
        dx, dy = gray(slot // SIDE), gray(slot % SIDE)
        return ((mx + dx) % SIDE) * SIDE + (my + dy) % SIDE

    def back_of(slot):
        dx, dy = gray(slot // SIDE), gray(slot % SIDE)
        return ((mx + SIDE - dx) % SIDE) * SIDE + (my + SIDE - dy) % SIDE

    barrier = pltpu.get_barrier_semaphore()
    for slot in range(1, ROWS):
        pl.semaphore_signal(barrier, inc=1, device_id={"passage": peer_of(slot)}, device_id_type=MESH)

    for step in (-1, 1):
        pl.semaphore_signal(barrier, inc=1, device_id=along(step), device_id_type=MESH)
    pl.semaphore_signal(barrier, inc=1, device_id=partner, device_id_type=MESH)
    for load in loads:
        load.start()

    def know_send(level):
        for side, step in enumerate((1, -1)):
            pl.semaphore_signal(
                tok.at[level, side], inc=1, device_id=along(step * (1 << level)), device_id_type=MESH
            )

    def know_wait(level):
        for side in range(2):
            pl.semaphore_wait(tok.at[level, side], 1)

    loads[0].wait()
    loads[1].wait()
    lane = lax.broadcasted_iota(jnp.int32, (8, 128), 1)
    row = lax.broadcasted_iota(jnp.int32, (block, block), 0)
    col = lax.broadcasted_iota(jnp.int32, (block, block), 1)
    order = jnp.where(col == (row % qcount) * qtok + row // qcount, 1.0, 0.0).astype(BF16)
    mine = jnp.dot(order, queries_ref[...].reshape(block, width), preferred_element_type=F32)
    qbuf[0:block, :] = mine.astype(BF16)

    listed = jnp.concatenate(
        [lists_ref[...].astype(F32), jnp.zeros((qcount, 128 - lists_ref.shape[1]), F32)], axis=1
    )
    listed = jnp.concatenate([listed, jnp.zeros((128 - qcount, 128), F32)], axis=0).T
    listed = listed[: lists_ref.shape[1], :]
    lrow = lax.broadcasted_iota(jnp.int32, (lists_ref.shape[1], 128), 1)
    number = jnp.where(lrow % 8 < pcount, (lrow // 8) * pcount + lrow % 8, -1).astype(F32)
    counts, firsts = [], []
    for query in range(qcount):
        hit = jnp.where(listed[:, query : query + 1] == number, 1.0, 0.0)
        counts.append(jnp.sum(hit, axis=0, keepdims=True))
        firsts.append(hit[0:1, :])
    tile = jnp.concatenate(counts + firsts, axis=0)
    meta[0] = jnp.concatenate([tile, jnp.zeros_like(tile)], axis=0).astype(BF16)

    pl.semaphore_wait(barrier, ROWS - 1 + 2 + 1)
    know_send(0)

    def query_copy(slot):
        return pltpu.make_async_remote_copy(
            src_ref=qbuf.at[pl.ds(0, block)],
            dst_ref=qbuf.at[pl.ds(slot * block, block)],
            send_sem=qs.at[slot], recv_sem=qr.at[slot],
            device_id={"passage": back_of(slot)}, device_id_type=MESH,
        )

    def meta_copy(slot):
        return pltpu.make_async_remote_copy(
            src_ref=meta.at[0], dst_ref=meta.at[slot],
            send_sem=ms.at[slot], recv_sem=mr.at[slot],
            device_id={"passage": back_of(slot)}, device_id_type=MESH,
        )

    def score_copy(slot):
        return pltpu.make_async_remote_copy(
            src_ref=score.at[0], dst_ref=score.at[slot],
            send_sem=ss.at[slot], recv_sem=sr.at[slot],
            device_id={"passage": back_of(slot)}, device_id_type=MESH,
        )

    for slot in range(1, ROWS):
        query_copy(slot).start()
    for slot in range(1, ROWS):
        meta_copy(slot).start()

    loads[2].wait()
    loads[3].wait()

    def project(chunk, carry):
        rows = pl.ds(chunk * (ptok // PARTS), ptok // PARTS)
        states = hidden_ref[rows].reshape(piece, hwidth)
        turned[chunk] = states
        flat = jnp.dot(states, proj_ref[...], preferred_element_type=F32)
        size = jnp.sqrt(jnp.sum(flat * flat, axis=1, keepdims=True) + EPS)
        one = flat / size
        norm[chunk] = jnp.broadcast_to(size, one.shape)
        unit[chunk] = one
        embed[chunk] = one.astype(BF16)
        return carry

    lax.fori_loop(0, PARTS, project, 0)
    know_wait(0)
    know_send(1)

    def score_pair(pair, found):
        @pl.when(pair > 0)
        def _():
            query_copy(2 * pair).wait_recv()

        query_copy(2 * pair + 1).wait_recv()
        start = pl.multiple_of(pair * 2 * block, 2 * block)
        both = qbuf[pl.ds(start, 2 * block), :]
        top = None
        for chunk in range(PARTS):
            sims = lax.dot_general(
                embed[chunk], both, (((1,), (1,)), ((), ())), preferred_element_type=F32
            )
            expo[pair, chunk] = sims
            most = jnp.max(sims.reshape(piece // 8, 8, 2 * block), axis=0)
            top = most if top is None else jnp.maximum(top, most)
        top = jnp.maximum(top, pltpu.roll(top, 4, 0))
        mass = jnp.zeros_like(top)
        for chunk in range(PARTS):
            raised = jnp.exp(BETA * (expo[pair, chunk].reshape(piece // 8, 8, 2 * block) - top[None]))
            expo[pair, chunk] = raised.reshape(piece, 2 * block)
            mass = mass + jnp.sum(raised, axis=0)
        mass = mass + pltpu.roll(mass, 4, 0)
        rsum[pair] = 1.0 / mass
        lse = jnp.log(mass) + BETA * top
        for which in range(2):
            summed = lse[:, which * block : (which + 1) * block]
            for step in (4, 8, 16, 32, 64):
                summed = summed + pltpu.roll(summed, step, 1)
            found = jnp.where(lane // 8 == peer_of(2 * pair + which), summed, found)
        return found

    found = lax.fori_loop(0, ROWS // 2, score_pair, jnp.zeros((8, 128), F32))
    score[0] = found / BETA

    for slot in range(1, ROWS):
        score_copy(slot).start()

    know_wait(1)
    know_send(2)
    for slot in range(ROWS):
        if slot:
            meta_copy(slot).wait_recv()
        mrows[pl.ds(pl.multiple_of(8 * peer_of(slot), 8), 8), :] = meta[slot].astype(F32)[0:8]
    mcols[...] = mrows[...].T

    top = jnp.full((8, 128), NEGBIG, F32)
    for slot in range(ROWS):
        if slot:
            score_copy(slot).wait_recv()
        count = mcols[pl.ds(pl.multiple_of(8 * peer_of(slot), 8), 8), :]
        top = jnp.maximum(top, jnp.where(count > 0, score[slot], NEGBIG))
    top = jnp.max(top, axis=0, keepdims=True)
    mass = jnp.zeros((8, 128), F32)
    shares = None
    for slot in range(ROWS):
        count = mcols[pl.ds(pl.multiple_of(8 * peer_of(slot), 8), 8), :]
        term = jnp.where(count > 0, count * jnp.exp(jnp.where(count > 0, score[slot], top) - top), 0.0)
        mass = mass + term
        if slot == 0:
            shares = term
    mass = jnp.sum(mass, axis=0, keepdims=True)
    top, mass = jnp.broadcast_to(top, (8, 128)), jnp.broadcast_to(mass, (8, 128))
    loss = jnp.log(mass) + top - pltpu.roll(top, 124, 1)
    loss = jnp.where(lane % 8 < 4, loss, pltpu.roll(loss, 4, 1))
    loss_ref[...] = spread(loss, lane, me)[0:1, :qcount]
    probs = shares / mass
    coef = (probs - pltpu.roll(probs, 124, 1)) / total
    coef = jnp.where(lane % 8 < 4, coef, pltpu.roll(coef, 4, 1))
    sub = lax.broadcasted_iota(jnp.int32, (8, 128), 0)
    coef = jnp.where(sub < 4, coef, pltpu.roll(coef, 4, 0))

    def make_scale(pair, carry):
        for which in range(2):
            wide = spread(coef, lane, peer_of(2 * pair + which))
            scale[pair, :, which * block : (which + 1) * block] = (
                wide * rsum[pair, :, which * block : (which + 1) * block]
            )
        return carry

    lax.fori_loop(0, ROWS // 2, make_scale, 0)

    def chunk_grad(chunk, carry):
        def pair_grad(pair, acc):
            spreads = expo[pair, chunk].reshape(piece // 8, 8, 2 * block)
            weight = (spreads * scale[pair][None]).reshape(piece, 2 * block).astype(BF16)
            start = pl.multiple_of(pair * 2 * block, 2 * block)
            return acc + jnp.dot(weight, qbuf[pl.ds(start, 2 * block), :], preferred_element_type=F32)

        d_embed = lax.fori_loop(0, ROWS // 2, pair_grad, jnp.zeros((piece, width), F32))
        one = unit[chunk]
        inner = jnp.sum(d_embed * one, axis=1, keepdims=True)
        d_flat = ((d_embed - one * inner) / norm[chunk]).astype(BF16)
        grown = lax.dot_general(
            turned[chunk], d_flat, (((0,), (0,)), ((), ())), preferred_element_type=F32
        ).reshape(part.shape)

        @pl.when(chunk == 0)
        def _():
            part[...] = grown

        @pl.when(chunk > 0)
        def _():
            part[...] += grown

        return carry

    lax.fori_loop(0, PARTS, chunk_grad, 0)

    pair_copy = pltpu.make_async_remote_copy(
        src_ref=part.at[:, 1 - core], dst_ref=precv,
        send_sem=ps.at[0], recv_sem=ps.at[1], device_id=partner, device_id_type=MESH,
    )
    pair_copy.start()
    pair_copy.wait_recv()
    rsend[...] = part[:, core] + precv[...]

    def grad_copy(slot):
        return pltpu.make_async_remote_copy(
            src_ref=rsend.at[back_of(slot)], dst_ref=rrecv.at[slot],
            send_sem=rs.at[slot], recv_sem=rr.at[slot],
            device_id={"passage": back_of(slot)}, device_id_type=MESH,
        )

    for slot in range(1, ROWS):
        grad_copy(slot).start()
    acc = rsend[me]
    for slot in range(1, ROWS):
        grad_copy(slot).wait_recv()
        acc = acc + rrecv[slot]
    zbuf[mz] = acc

    def z_copy(step):
        return pltpu.make_async_remote_copy(
            src_ref=zbuf.at[mz], dst_ref=zbuf.at[mz],
            send_sem=zs.at[step], recv_sem=zr.at[step],
            device_id={"query": ((mz + step) % nz) * 2 + core}, device_id_type=MESH,
        )

    def z_arrival(step):
        source = (mz + nz - step) % nz
        return pltpu.make_async_remote_copy(
            src_ref=zbuf.at[source], dst_ref=zbuf.at[source],
            send_sem=zs.at[step], recv_sem=zr.at[step],
            device_id={"query": ((mz + step) % nz) * 2 + core}, device_id_type=MESH,
        )

    know_wait(2)
    for step in range(1, nz):
        z_copy(step).start()
    for step in range(1, nz):
        z_arrival(step).wait_recv()
    acc = zbuf[0]
    for step in range(1, nz):
        acc = acc + zbuf[step]
    fin[core] = acc
    fin_copy = pltpu.make_async_remote_copy(
        src_ref=fin.at[core], dst_ref=fin.at[core],
        send_sem=fs.at[0], recv_sem=fs.at[1], device_id=partner, device_id_type=MESH,
    )
    fin_copy.start()
    for slot in range(1, ROWS):
        query_copy(slot).wait_send()
        meta_copy(slot).wait_send()
        score_copy(slot).wait_send()
        grad_copy(slot).wait_send()
    pair_copy.wait_send()
    for step in range(1, nz):
        z_copy(step).wait_send()
    fin_arrival = pltpu.make_async_remote_copy(
        src_ref=fin.at[1 - core], dst_ref=fin.at[1 - core],
        send_sem=fs.at[0], recv_sem=fs.at[1], device_id=partner, device_id_type=MESH,
    )
    fin_arrival.wait_recv()
    fin_copy.wait_send()
    grad_ref[...] = fin[...].reshape(grad_ref.shape)


def body(queries, hidden, proj, lists):
    qcount, qtok, width = queries.shape
    pcount, ptok, hwidth = hidden.shape
    nside = lax.axis_size("passage")
    nq = lax.axis_size("query")
    total = qcount * nq * nside
    share = hwidth // nside
    piece = ptok * pcount // PARTS
    block = qcount * qtok
    pairs = nside // 2
    nz = nq // 2
    dma = pltpu.SemaphoreType.DMA
    losses, grad = pl.pallas_call(
        functools.partial(kernel, total),
        out_shape=(
            jax.ShapeDtypeStruct((1, qcount), F32),
            jax.ShapeDtypeStruct((share, width), F32),
        ),
        in_specs=[pl.BlockSpec(memory_space=pl.ANY)] * 4,
        out_specs=(pl.BlockSpec(memory_space=pltpu.VMEM),) * 2,
        scratch_shapes=[
            pltpu.VMEM(queries.shape, BF16),
            pltpu.VMEM((ptok, pcount, hwidth), BF16),
            pltpu.VMEM(proj.shape, BF16),
            pltpu.VMEM(lists.shape, lists.dtype),
            pltpu.VMEM((nside * block, width), BF16),
            pltpu.VMEM((nside, 16, 128), BF16),
            pltpu.VMEM((128, 128), F32),
            pltpu.VMEM((128, 128), F32),
            pltpu.VMEM((PARTS, piece, hwidth), BF16),
            pltpu.VMEM((PARTS, piece, width), BF16),
            pltpu.VMEM((PARTS, piece, width), F32),
            pltpu.VMEM((PARTS, piece, width), F32),
            pltpu.VMEM((pairs, PARTS, piece, 2 * block), F32),
            pltpu.VMEM((pairs, 8, 2 * block), F32),
            pltpu.VMEM((nside, 8, 128), F32),
            pltpu.VMEM((pairs, 8, 2 * block), F32),
            pltpu.VMEM((nside, 2, share // 2, width), F32),
            pltpu.VMEM((nside, share // 2, width), F32),
            pltpu.VMEM((nside, share // 2, width), F32),
            pltpu.VMEM((nside, share // 2, width), F32),
            pltpu.VMEM((nz, share // 2, width), F32),
            pltpu.VMEM((2, share // 2, width), F32),
            dma((4,)),
            dma((nside,)), dma((nside,)),
            dma((nside,)), dma((nside,)),
            dma((nside,)), dma((nside,)),
            dma((2,)),
            dma((nside,)), dma((nside,)),
            dma((nz,)), dma((nz,)),
            dma((2,)),
            pltpu.SemaphoreType.REGULAR((3, 2)),
        ],
        compiler_params=pltpu.CompilerParams(
            collective_id=0, has_side_effects=True, vmem_limit_bytes=60 * 1024 * 1024
        ),
        name="retriever_step",
    )(queries, hidden.transpose(1, 0, 2), proj, lists)
    return (losses.reshape(qcount), grad)


def solution(mesh):
    placed = (
        P(("query", "passage"), None, None),
        P(("query", "passage"), None, None),
        P(),
        P(("query", "passage"), None),
    )
    return jax.shard_map(
        body,
        mesh=mesh,
        in_specs=placed,
        out_specs=(P(("query", "passage")), P("passage", None)),
        check_vma=False,
    )
```

```python
import functools
import math

import jax
import jax.numpy as jnp
from jax import lax
from jax.experimental import pallas as pl
from jax.experimental.pallas import tpu as pltpu
from jax.sharding import PartitionSpec as P

BETA = 4.0
BETA2 = BETA * math.log2(math.e)
EPS = 1e-06
SIDE = 4
ROWS = SIDE * SIDE
F32 = jnp.float32
BF16 = jnp.bfloat16
NEGBIG = -3.0e38
PARTS = 3
MESH = pl.DeviceIdType.MESH


def gray(index):
    return index ^ (index >> 1)


def spread(tile, lane, block):
    own = jnp.where(lane // 8 == block, tile, 0.0)
    for step in (8, 16, 32, 64):
        own = own + pltpu.roll(own, step, 1)
    return own


def kernel(
    total,
    queries_hbm, hidden_hbm, proj_hbm, lists_hbm,
    loss_ref, grad_ref,
    queries_ref, hidden_ref, proj_ref, lists_ref,
    qbuf, meta, mrows, mcols, turned, embed, unit, norm, expo, rsum, score, scale, d_flat,
    part, precv, rsend, rrecv, zbuf, fin,
    ins, qs, qr, ms, mr, ss, sr, ps, rs, rr, zs, zr, fs, tok,
):
    qcount, qtok, width = queries_ref.shape
    ptok, pcount, hwidth = hidden_ref.shape
    nz = lax.axis_size("query") // 2
    qid = lax.axis_index("query")
    me = lax.axis_index("passage")
    mx, my = me // SIDE, me % SIDE
    mz, core = qid // 2, qid % 2
    partner = {"query": mz * 2 + (1 - core)}
    block = qcount * qtok
    half = grad_ref.shape[0] // 2
    piece = ptok * pcount // PARTS

    def along(step):
        return {"query": ((mz + nz + step) % nz) * 2 + core}

    loads = [
        pltpu.make_async_copy(src, dst, ins.at[n])
        for n, (src, dst) in enumerate(
            [(queries_hbm, queries_ref), (lists_hbm, lists_ref), (proj_hbm, proj_ref), (hidden_hbm, hidden_ref)]
        )
    ]

    def peer_of(slot):
        dx, dy = gray(slot // SIDE), gray(slot % SIDE)
        return ((mx + dx) % SIDE) * SIDE + (my + dy) % SIDE

    def back_of(slot):
        dx, dy = gray(slot // SIDE), gray(slot % SIDE)
        return ((mx + SIDE - dx) % SIDE) * SIDE + (my + SIDE - dy) % SIDE

    barrier = pltpu.get_barrier_semaphore()
    for slot in range(1, ROWS):
        pl.semaphore_signal(barrier, inc=1, device_id={"passage": peer_of(slot)}, device_id_type=MESH)

    for step in (-1, 1):
        pl.semaphore_signal(barrier, inc=1, device_id=along(step), device_id_type=MESH)
    pl.semaphore_signal(barrier, inc=1, device_id=partner, device_id_type=MESH)
    for load in loads:
        load.start()

    def know_send(level):
        for side, step in enumerate((1, -1)):
            pl.semaphore_signal(
                tok.at[level, side], inc=1, device_id=along(step * (1 << level)), device_id_type=MESH
            )

    def know_wait(level):
        for side in range(2):
            pl.semaphore_wait(tok.at[level, side], 1)

    loads[0].wait()
    loads[1].wait()
    lane = lax.broadcasted_iota(jnp.int32, (8, 128), 1)
    row = lax.broadcasted_iota(jnp.int32, (block, block), 0)
    col = lax.broadcasted_iota(jnp.int32, (block, block), 1)
    order = jnp.where(col == (row % qcount) * qtok + row // qcount, 1.0, 0.0).astype(BF16)
    mine = jnp.dot(order, queries_ref[...].reshape(block, width), preferred_element_type=F32)
    qbuf[0:block, :] = mine.astype(BF16)

    listed = jnp.concatenate(
        [lists_ref[...].astype(F32), jnp.zeros((qcount, 128 - lists_ref.shape[1]), F32)], axis=1
    )
    listed = jnp.concatenate([listed, jnp.zeros((128 - qcount, 128), F32)], axis=0).T
    listed = listed[: lists_ref.shape[1], :]
    lrow = lax.broadcasted_iota(jnp.int32, (lists_ref.shape[1], 128), 1)
    number = jnp.where(lrow % 8 < pcount, (lrow // 8) * pcount + lrow % 8, -1).astype(F32)
    counts, firsts = [], []
    for query in range(qcount):
        hit = jnp.where(listed[:, query : query + 1] == number, 1.0, 0.0)
        counts.append(jnp.sum(hit, axis=0, keepdims=True))
        firsts.append(hit[0:1, :])
    tile = jnp.concatenate(counts + firsts, axis=0)
    meta[0] = jnp.concatenate([tile, jnp.zeros_like(tile)], axis=0).astype(BF16)

    pl.semaphore_wait(barrier, ROWS - 1 + 2 + 1)
    know_send(0)

    def query_copy(slot):
        return pltpu.make_async_remote_copy(
            src_ref=qbuf.at[pl.ds(0, block)],
            dst_ref=qbuf.at[pl.ds(slot * block, block)],
            send_sem=qs.at[slot], recv_sem=qr.at[slot],
            device_id={"passage": back_of(slot)}, device_id_type=MESH,
        )

    def meta_copy(slot):
        return pltpu.make_async_remote_copy(
            src_ref=meta.at[0], dst_ref=meta.at[slot],
            send_sem=ms.at[slot], recv_sem=mr.at[slot],
            device_id={"passage": back_of(slot)}, device_id_type=MESH,
        )

    def score_copy(slot):
        return pltpu.make_async_remote_copy(
            src_ref=score.at[0], dst_ref=score.at[slot],
            send_sem=ss.at[slot], recv_sem=sr.at[slot],
            device_id={"passage": back_of(slot)}, device_id_type=MESH,
        )

    for slot in range(1, ROWS):
        query_copy(slot).start()
    for slot in range(1, ROWS):
        meta_copy(slot).start()

    loads[2].wait()
    loads[3].wait()

    def project(chunk, carry):
        rows = pl.ds(chunk * (ptok // PARTS), ptok // PARTS)
        states = hidden_ref[rows].reshape(piece, hwidth)
        turned[chunk] = states.T
        flat = jnp.dot(states, proj_ref[...], preferred_element_type=F32)
        size = jnp.sqrt(jnp.sum(flat * flat, axis=1, keepdims=True) + EPS)
        one = flat / size
        norm[chunk] = jnp.broadcast_to(size, one.shape)
        unit[chunk] = one
        embed[chunk] = one.astype(BF16)
        return carry

    lax.fori_loop(0, PARTS, project, 0)
    know_wait(0)
    know_send(1)

    def score_pair(pair, found):
        @pl.when(pair > 0)
        def _():
            query_copy(2 * pair).wait_recv()

        query_copy(2 * pair + 1).wait_recv()
        start = pl.multiple_of(pair * 2 * block, 2 * block)
        both = qbuf[pl.ds(start, 2 * block), :]
        top = None
        for chunk in range(PARTS):
            sims = lax.dot_general(
                embed[chunk], both, (((1,), (1,)), ((), ())), preferred_element_type=F32
            )
            expo[pair, chunk] = sims
            most = jnp.max(sims.reshape(piece // 8, 8, 2 * block), axis=0)
            top = most if top is None else jnp.maximum(top, most)
        top = jnp.maximum(top, pltpu.roll(top, 4, 0))
        mass = jnp.zeros_like(top)
        for chunk in range(PARTS):
            raised = jnp.exp2(BETA2 * (expo[pair, chunk].reshape(piece // 8, 8, 2 * block) - top[None]))
            expo[pair, chunk] = raised.reshape(piece, 2 * block)
            mass = mass + jnp.sum(raised, axis=0)
        mass = mass + pltpu.roll(mass, 4, 0)
        rsum[pair] = 1.0 / mass
        lse = jnp.log(mass) + BETA * top
        for which in range(2):
            summed = lse[:, which * block : (which + 1) * block]
            for step in (4, 8, 16, 32, 64):
                summed = summed + pltpu.roll(summed, step, 1)
            found = jnp.where(lane // 8 == peer_of(2 * pair + which), summed, found)
        return found

    found = lax.fori_loop(0, ROWS // 2, score_pair, jnp.zeros((8, 128), F32))
    score[0] = found / BETA

    for slot in range(1, ROWS):
        score_copy(slot).start()

    know_wait(1)
    know_send(2)
    for slot in range(ROWS):
        if slot:
            meta_copy(slot).wait_recv()
        mrows[pl.ds(pl.multiple_of(8 * peer_of(slot), 8), 8), :] = meta[slot].astype(F32)[0:8]
    mcols[...] = mrows[...].T

    top = jnp.full((8, 128), NEGBIG, F32)
    for slot in range(ROWS):
        if slot:
            score_copy(slot).wait_recv()
        count = mcols[pl.ds(pl.multiple_of(8 * peer_of(slot), 8), 8), :]
        top = jnp.maximum(top, jnp.where(count > 0, score[slot], NEGBIG))
    top = jnp.max(top, axis=0, keepdims=True)
    mass = jnp.zeros((8, 128), F32)
    shares = None
    for slot in range(ROWS):
        count = mcols[pl.ds(pl.multiple_of(8 * peer_of(slot), 8), 8), :]
        term = jnp.where(count > 0, count * jnp.exp(jnp.where(count > 0, score[slot], top) - top), 0.0)
        mass = mass + term
        if slot == 0:
            shares = term
    mass = jnp.sum(mass, axis=0, keepdims=True)
    top, mass = jnp.broadcast_to(top, (8, 128)), jnp.broadcast_to(mass, (8, 128))
    loss = jnp.log(mass) + top - pltpu.roll(top, 124, 1)
    loss = jnp.where(lane % 8 < 4, loss, pltpu.roll(loss, 4, 1))
    loss_ref[...] = spread(loss, lane, me)[0:1, :qcount]
    probs = shares / mass
    coef = (probs - pltpu.roll(probs, 124, 1)) / total
    coef = jnp.where(lane % 8 < 4, coef, pltpu.roll(coef, 4, 1))
    sub = lax.broadcasted_iota(jnp.int32, (8, 128), 0)
    coef = jnp.where(sub < 4, coef, pltpu.roll(coef, 4, 0))

    for pair in range(ROWS // 2):
        for which in range(2):
            wide = spread(coef, lane, peer_of(2 * pair + which))
            scale[pair, :, which * block : (which + 1) * block] = (
                wide * rsum[pair, :, which * block : (which + 1) * block]
            )

    def chunk_grad(chunk, carry):
        d_embed = None
        for pair in range(ROWS // 2):
            spreads = expo[pair, chunk].reshape(piece // 8, 8, 2 * block)
            weight = (spreads * scale[pair][None]).reshape(piece, 2 * block).astype(BF16)
            term = jnp.dot(
                weight, qbuf[pair * 2 * block : (pair + 1) * 2 * block, :], preferred_element_type=F32
            )
            d_embed = term if d_embed is None else d_embed + term
        one = unit[chunk]
        inner = jnp.sum(d_embed * one, axis=1, keepdims=True)
        d_flat[chunk] = ((d_embed - one * inner) / norm[chunk]).astype(BF16)
        return carry

    lax.fori_loop(0, PARTS, chunk_grad, 0)
    grown = None
    for chunk in range(PARTS):
        term = jnp.dot(turned[chunk], d_flat[chunk], preferred_element_type=F32)
        grown = term if grown is None else grown + term
    part[...] = grown.reshape(part.shape)

    def pair_copy(ix):
        line = pl.ds(((mx + SIDE - gray(ix)) % SIDE) * SIDE, SIDE)
        return pltpu.make_async_remote_copy(
            src_ref=part.at[line, 1 - core], dst_ref=precv.at[line],
            send_sem=ps.at[0, ix], recv_sem=ps.at[1, ix], device_id=partner, device_id_type=MESH,
        )

    for ix in (3, 2, 1, 0):
        pair_copy(ix).start()

    def grad_copy(slot):
        return pltpu.make_async_remote_copy(
            src_ref=rsend.at[back_of(slot)], dst_ref=rrecv.at[slot],
            send_sem=rs.at[slot], recv_sem=rr.at[slot],
            device_id={"passage": back_of(slot)}, device_id_type=MESH,
        )

    for ix in (3, 2, 1, 0):
        line = pl.ds(((mx + SIDE - gray(ix)) % SIDE) * SIDE, SIDE)
        pair_copy(ix).wait_recv()
        rsend[line] = part[line, core] + precv[line]
        for iy in (3, 2, 1, 0):
            if ix or iy:
                grad_copy(ix * SIDE + iy).start()
    acc = rsend[me]
    for slot in range(1, ROWS):
        grad_copy(slot).wait_recv()
        acc = acc + rrecv[slot]
    zbuf[mz] = acc

    def z_copy(step):
        return pltpu.make_async_remote_copy(
            src_ref=zbuf.at[mz], dst_ref=zbuf.at[mz],
            send_sem=zs.at[step], recv_sem=zr.at[step],
            device_id={"query": ((mz + step) % nz) * 2 + core}, device_id_type=MESH,
        )

    def z_arrival(step):
        source = (mz + nz - step) % nz
        return pltpu.make_async_remote_copy(
            src_ref=zbuf.at[source], dst_ref=zbuf.at[source],
            send_sem=zs.at[step], recv_sem=zr.at[step],
            device_id={"query": ((mz + step) % nz) * 2 + core}, device_id_type=MESH,
        )

    know_wait(2)
    for step in range(1, nz):
        z_copy(step).start()
    for step in range(1, nz):
        z_arrival(step).wait_recv()
    acc = zbuf[0]
    for step in range(1, nz):
        acc = acc + zbuf[step]
    fin[core] = acc
    fin_copy = pltpu.make_async_remote_copy(
        src_ref=fin.at[core], dst_ref=fin.at[core],
        send_sem=fs.at[0], recv_sem=fs.at[1], device_id=partner, device_id_type=MESH,
    )
    fin_copy.start()
    for slot in range(1, ROWS):
        query_copy(slot).wait_send()
        meta_copy(slot).wait_send()
        score_copy(slot).wait_send()
        grad_copy(slot).wait_send()
    for ix in range(SIDE):
        pair_copy(ix).wait_send()
    for step in range(1, nz):
        z_copy(step).wait_send()
    fin_arrival = pltpu.make_async_remote_copy(
        src_ref=fin.at[1 - core], dst_ref=fin.at[1 - core],
        send_sem=fs.at[0], recv_sem=fs.at[1], device_id=partner, device_id_type=MESH,
    )
    fin_arrival.wait_recv()
    fin_copy.wait_send()
    grad_ref[...] = fin[...].reshape(grad_ref.shape)


def hand_over(loss_in, grad_in, loss_ref, grad_ref):
    loss_ref[...] = loss_in[...]
    grad_ref[...] = grad_in[...]


def body(queries, hidden, proj, lists):
    qcount, qtok, width = queries.shape
    pcount, ptok, hwidth = hidden.shape
    nside = lax.axis_size("passage")
    nq = lax.axis_size("query")
    total = qcount * nq * nside
    share = hwidth // nside
    piece = ptok * pcount // PARTS
    block = qcount * qtok
    pairs = nside // 2
    nz = nq // 2
    dma = pltpu.SemaphoreType.DMA
    losses, grad = pl.pallas_call(
        functools.partial(kernel, total),
        out_shape=(
            jax.ShapeDtypeStruct((1, qcount), F32),
            jax.ShapeDtypeStruct((share, width), F32),
        ),
        in_specs=[pl.BlockSpec(memory_space=pl.ANY)] * 4,
        out_specs=(pl.BlockSpec(memory_space=pltpu.VMEM),) * 2,
        scratch_shapes=[
            pltpu.VMEM(queries.shape, BF16),
            pltpu.VMEM((ptok, pcount, hwidth), BF16),
            pltpu.VMEM(proj.shape, BF16),
            pltpu.VMEM(lists.shape, lists.dtype),
            pltpu.VMEM((nside * block, width), BF16),
            pltpu.VMEM((nside, 16, 128), BF16),
            pltpu.VMEM((128, 128), F32),
            pltpu.VMEM((128, 128), F32),
            pltpu.VMEM((PARTS, hwidth, piece), BF16),
            pltpu.VMEM((PARTS, piece, width), BF16),
            pltpu.VMEM((PARTS, piece, width), F32),
            pltpu.VMEM((PARTS, piece, width), F32),
            pltpu.VMEM((pairs, PARTS, piece, 2 * block), F32),
            pltpu.VMEM((pairs, 8, 2 * block), F32),
            pltpu.VMEM((nside, 8, 128), F32),
            pltpu.VMEM((pairs, 8, 2 * block), F32),
            pltpu.VMEM((PARTS, piece, width), BF16),
            pltpu.VMEM((nside, 2, share // 2, width), F32),
            pltpu.VMEM((nside, share // 2, width), F32),
            pltpu.VMEM((nside, share // 2, width), F32),
            pltpu.VMEM((nside, share // 2, width), F32),
            pltpu.VMEM((nz, share // 2, width), F32),
            pltpu.VMEM((2, share // 2, width), F32),
            dma((4,)),
            dma((nside,)), dma((nside,)),
            dma((nside,)), dma((nside,)),
            dma((nside,)), dma((nside,)),
            dma((2, SIDE)),
            dma((nside,)), dma((nside,)),
            dma((nz,)), dma((nz,)),
            dma((2,)),
            pltpu.SemaphoreType.REGULAR((3, 2)),
        ],
        compiler_params=pltpu.CompilerParams(
            collective_id=0, has_side_effects=True, vmem_limit_bytes=60 * 1024 * 1024
        ),
        name="retriever_step",
    )(queries, hidden.transpose(1, 0, 2), proj, lists)
    losses, grad = pl.pallas_call(
        hand_over,
        out_shape=(
            jax.ShapeDtypeStruct((1, qcount), F32),
            jax.ShapeDtypeStruct((share, width), F32),
        ),
        in_specs=[pl.BlockSpec(memory_space=pltpu.VMEM)] * 2,
        out_specs=(pl.BlockSpec(memory_space=pltpu.VMEM),) * 2,
        name="outputs",
    )(losses, grad)
    return (losses.reshape(qcount), grad)


def solution(mesh):
    placed = (
        P(("query", "passage"), None, None),
        P(("query", "passage"), None, None),
        P(),
        P(("query", "passage"), None),
    )
    return jax.shard_map(
        body,
        mesh=mesh,
        in_specs=placed,
        out_specs=(P(("query", "passage")), P("passage", None)),
        check_vma=False,
    )
```

```python
import functools
import math

import jax
import jax.numpy as jnp
from jax import lax
from jax.experimental import pallas as pl
from jax.experimental.pallas import tpu as pltpu
from jax.sharding import PartitionSpec as P

BETA = 4.0
BETA2 = BETA * math.log2(math.e)
EPS = 1e-06
SIDE = 4
ROWS = SIDE * SIDE
F32 = jnp.float32
BF16 = jnp.bfloat16
NEGBIG = -3.0e38
PARTS = 3
MESH = pl.DeviceIdType.MESH


def gray(index):
    return index ^ (index >> 1)


def spread(tile, lane, block):
    own = jnp.where(lane // 8 == block, tile, 0.0)
    for step in (8, 16, 32, 64):
        own = own + pltpu.roll(own, step, 1)
    return own


def kernel(
    total,
    queries_hbm, hidden_hbm, proj_hbm, lists_hbm,
    loss_ref, grad_ref,
    queries_ref, hidden_ref, proj_ref, lists_ref,
    qbuf, meta, mrows, mcols, turned, embed, unit, norm, expo, rsum, tops, score, scale, d_flat,
    part, given, precv, own, rsend, rrecv, zbuf, fin,
    ins, qs, qr, ms, mr, ss, sr, ps, rs, rr, zs, zr, fs, tok,
):
    qcount, qtok, width = queries_ref.shape
    ptok, pcount, hwidth = hidden_ref.shape
    nz = lax.axis_size("query") // 2
    qid = lax.axis_index("query")
    me = lax.axis_index("passage")
    mx, my = me // SIDE, me % SIDE
    mz, core = qid // 2, qid % 2
    partner = {"query": mz * 2 + (1 - core)}
    block = qcount * qtok
    half = grad_ref.shape[0] // 2
    piece = ptok * pcount // PARTS

    def along(step):
        return {"query": ((mz + nz + step) % nz) * 2 + core}

    loads = [
        pltpu.make_async_copy(src, dst, ins.at[n])
        for n, (src, dst) in enumerate(
            [(queries_hbm, queries_ref), (lists_hbm, lists_ref), (proj_hbm, proj_ref), (hidden_hbm, hidden_ref)]
        )
    ]

    def peer_of(slot):
        dx, dy = gray(slot // SIDE), gray(slot % SIDE)
        return ((mx + dx) % SIDE) * SIDE + (my + dy) % SIDE

    def back_of(slot):
        dx, dy = gray(slot // SIDE), gray(slot % SIDE)
        return ((mx + SIDE - dx) % SIDE) * SIDE + (my + SIDE - dy) % SIDE

    barrier = pltpu.get_barrier_semaphore()
    for slot in range(1, ROWS):
        pl.semaphore_signal(barrier, inc=1, device_id={"passage": peer_of(slot)}, device_id_type=MESH)

    for step in (-1, 1):
        pl.semaphore_signal(barrier, inc=1, device_id=along(step), device_id_type=MESH)
    pl.semaphore_signal(barrier, inc=1, device_id=partner, device_id_type=MESH)
    for load in loads:
        load.start()

    def know_send(level):
        for side, step in enumerate((1, -1)):
            pl.semaphore_signal(
                tok.at[level, side], inc=1, device_id=along(step * (1 << level)), device_id_type=MESH
            )

    def know_wait(level):
        for side in range(2):
            pl.semaphore_wait(tok.at[level, side], 1)

    loads[0].wait()
    loads[1].wait()
    lane = lax.broadcasted_iota(jnp.int32, (8, 128), 1)
    row = lax.broadcasted_iota(jnp.int32, (block, block), 0)
    col = lax.broadcasted_iota(jnp.int32, (block, block), 1)
    order = jnp.where(col == (row % qcount) * qtok + row // qcount, 1.0, 0.0).astype(BF16)
    mine = jnp.dot(order, queries_ref[...].reshape(block, width), preferred_element_type=F32)
    qbuf[0:block, :] = mine.astype(BF16)

    listed = jnp.concatenate(
        [lists_ref[...].astype(F32), jnp.zeros((qcount, 128 - lists_ref.shape[1]), F32)], axis=1
    )
    listed = jnp.concatenate([listed, jnp.zeros((128 - qcount, 128), F32)], axis=0).T
    listed = listed[: lists_ref.shape[1], :]
    lrow = lax.broadcasted_iota(jnp.int32, (lists_ref.shape[1], 128), 1)
    number = jnp.where(lrow % 8 < pcount, (lrow // 8) * pcount + lrow % 8, -1).astype(F32)
    counts, firsts = [], []
    for query in range(qcount):
        hit = jnp.where(listed[:, query : query + 1] == number, 1.0, 0.0)
        counts.append(jnp.sum(hit, axis=0, keepdims=True))
        firsts.append(hit[0:1, :])
    tile = jnp.concatenate(counts + firsts, axis=0)
    meta[0] = tile.astype(BF16)

    pl.semaphore_wait(barrier, ROWS - 1 + 2 + 1)
    know_send(0)

    def query_copy(slot):
        return pltpu.make_async_remote_copy(
            src_ref=qbuf.at[pl.ds(0, block)],
            dst_ref=qbuf.at[pl.ds(slot * block, block)],
            send_sem=qs.at[slot], recv_sem=qr.at[slot],
            device_id={"passage": back_of(slot)}, device_id_type=MESH,
        )

    def meta_copy(slot):
        return pltpu.make_async_remote_copy(
            src_ref=meta.at[0], dst_ref=meta.at[slot],
            send_sem=ms.at[slot], recv_sem=mr.at[slot],
            device_id={"passage": back_of(slot)}, device_id_type=MESH,
        )

    def score_copy(slot):
        return pltpu.make_async_remote_copy(
            src_ref=score.at[0], dst_ref=score.at[slot],
            send_sem=ss.at[slot], recv_sem=sr.at[slot],
            device_id={"passage": back_of(slot)}, device_id_type=MESH,
        )

    for slot in range(1, ROWS):
        query_copy(slot).start()
    for slot in range(1, ROWS):
        meta_copy(slot).start()

    loads[2].wait()
    loads[3].wait()

    def project(chunk, carry):
        rows = pl.ds(chunk * (ptok // PARTS), ptok // PARTS)
        states = hidden_ref[rows].reshape(piece, hwidth)
        turned[chunk] = states.T
        flat = jnp.dot(states, proj_ref[...], preferred_element_type=F32)
        size = jnp.sqrt(jnp.sum(flat * flat, axis=1, keepdims=True) + EPS)
        one = flat / size
        norm[chunk] = jnp.broadcast_to(size, one.shape)
        unit[chunk] = one
        embed[chunk] = one.astype(BF16)
        return carry

    lax.fori_loop(0, PARTS, project, 0)
    know_wait(0)
    know_send(1)

    def score_pair(pair, carry):
        @pl.when(pair > 0)
        def _():
            query_copy(2 * pair).wait_recv()

        query_copy(2 * pair + 1).wait_recv()
        start = pl.multiple_of(pair * 2 * block, 2 * block)
        both = qbuf[pl.ds(start, 2 * block), :]
        top = None
        for chunk in range(PARTS):
            sims = lax.dot_general(
                embed[chunk], both, (((1,), (1,)), ((), ())), preferred_element_type=F32
            )
            expo[pair, chunk] = sims
            most = jnp.max(sims.reshape(piece // 8, 8, 2 * block), axis=0)
            top = most if top is None else jnp.maximum(top, most)
        top = jnp.maximum(top, pltpu.roll(top, 4, 0))
        mass = jnp.zeros_like(top)
        for chunk in range(PARTS):
            raised = jnp.exp2(BETA2 * (expo[pair, chunk].reshape(piece // 8, 8, 2 * block) - top[None]))
            expo[pair, chunk] = raised.reshape(piece, 2 * block)
            mass = mass + jnp.sum(raised, axis=0)
        mass = mass + pltpu.roll(mass, 4, 0)
        rsum[pair] = mass
        tops[pair] = top
        return carry

    lax.fori_loop(0, ROWS // 2, score_pair, 0)
    found = jnp.zeros((8, 128), F32)
    for pair in range(ROWS // 2):
        lse = jnp.log(rsum[pair]) + BETA * tops[pair]
        for which in range(2):
            summed = lse[:, which * block : (which + 1) * block]
            for step in (4, 8, 16, 32, 64):
                summed = summed + pltpu.roll(summed, step, 1)
            found = jnp.where(lane // 8 == peer_of(2 * pair + which), summed, found)
    score[0] = found / BETA

    for slot in range(1, ROWS):
        score_copy(slot).start()

    know_wait(1)
    know_send(2)
    for slot in range(ROWS):
        if slot:
            meta_copy(slot).wait_recv()
        mrows[pl.ds(pl.multiple_of(8 * peer_of(slot), 8), 8), :] = meta[slot].astype(F32)
    mcols[...] = mrows[...].T

    top = jnp.full((8, 128), NEGBIG, F32)
    for slot in range(ROWS):
        if slot:
            score_copy(slot).wait_recv()
        count = mcols[pl.ds(pl.multiple_of(8 * peer_of(slot), 8), 8), :]
        top = jnp.maximum(top, jnp.where(count > 0, score[slot], NEGBIG))
    top = jnp.max(top, axis=0, keepdims=True)
    mass = jnp.zeros((8, 128), F32)
    shares = None
    for slot in range(ROWS):
        count = mcols[pl.ds(pl.multiple_of(8 * peer_of(slot), 8), 8), :]
        term = jnp.where(count > 0, count * jnp.exp(jnp.where(count > 0, score[slot], top) - top), 0.0)
        mass = mass + term
        if slot == 0:
            shares = term
    mass = jnp.sum(mass, axis=0, keepdims=True)
    top, mass = jnp.broadcast_to(top, (8, 128)), jnp.broadcast_to(mass, (8, 128))
    loss = jnp.log(mass) + top - pltpu.roll(top, 124, 1)
    loss = jnp.where(lane % 8 < 4, loss, pltpu.roll(loss, 4, 1))
    loss_ref[...] = spread(loss, lane, me)[0:1, :qcount]
    probs = shares / mass
    coef = (probs - pltpu.roll(probs, 124, 1)) / total
    coef = jnp.where(lane % 8 < 4, coef, pltpu.roll(coef, 4, 1))
    sub = lax.broadcasted_iota(jnp.int32, (8, 128), 0)
    coef = jnp.where(sub < 4, coef, pltpu.roll(coef, 4, 0))

    for pair in range(ROWS // 2):
        for which in range(2):
            wide = spread(coef, lane, peer_of(2 * pair + which))
            scale[pair, :, which * block : (which + 1) * block] = (
                wide / rsum[pair, :, which * block : (which + 1) * block]
            )

    def chunk_grad(chunk, carry):
        d_embed = None
        for pair in range(ROWS // 2):
            spreads = expo[pair, chunk].reshape(piece // 8, 8, 2 * block)
            weight = (spreads * scale[pair][None]).reshape(piece, 2 * block).astype(BF16)
            term = jnp.dot(
                weight, qbuf[pair * 2 * block : (pair + 1) * 2 * block, :], preferred_element_type=F32
            )
            d_embed = term if d_embed is None else d_embed + term
        one = unit[chunk]
        inner = jnp.sum(d_embed * one, axis=1, keepdims=True)
        d_flat[chunk] = ((d_embed - one * inner) / norm[chunk]).astype(BF16)
        return carry

    lax.fori_loop(0, PARTS, chunk_grad, 0)
    grown = None
    for chunk in range(PARTS):
        term = jnp.dot(turned[chunk], d_flat[chunk], preferred_element_type=F32)
        grown = term if grown is None else grown + term
    part[...] = grown.reshape(part.shape)
    given[...] = part[:, 1 - core].astype(BF16)

    def pair_copy(ix):
        line = pl.ds(((mx + SIDE - gray(ix)) % SIDE) * SIDE, SIDE)
        return pltpu.make_async_remote_copy(
            src_ref=given.at[line], dst_ref=precv.at[line],
            send_sem=ps.at[0, ix], recv_sem=ps.at[1, ix], device_id=partner, device_id_type=MESH,
        )

    for ix in (3, 2, 1, 0):
        pair_copy(ix).start()

    def grad_copy(slot):
        return pltpu.make_async_remote_copy(
            src_ref=rsend.at[back_of(slot)], dst_ref=rrecv.at[slot],
            send_sem=rs.at[slot], recv_sem=rr.at[slot],
            device_id={"passage": back_of(slot)}, device_id_type=MESH,
        )

    for ix in (3, 2, 1, 0):
        line = pl.ds(((mx + SIDE - gray(ix)) % SIDE) * SIDE, SIDE)
        pair_copy(ix).wait_recv()
        own[line] = part[line, core] + precv[line].astype(F32)
        rsend[line] = own[line].astype(BF16)
        for iy in (3, 2, 1, 0):
            if ix or iy:
                grad_copy(ix * SIDE + iy).start()
    acc = own[me]
    for slot in range(1, ROWS):
        grad_copy(slot).wait_recv()
        acc = acc + rrecv[slot].astype(F32)
    zbuf[mz] = acc.astype(BF16)

    def z_copy(step):
        return pltpu.make_async_remote_copy(
            src_ref=zbuf.at[mz], dst_ref=zbuf.at[mz],
            send_sem=zs.at[step], recv_sem=zr.at[step],
            device_id={"query": ((mz + step) % nz) * 2 + core}, device_id_type=MESH,
        )

    def z_arrival(step):
        source = (mz + nz - step) % nz
        return pltpu.make_async_remote_copy(
            src_ref=zbuf.at[source], dst_ref=zbuf.at[source],
            send_sem=zs.at[step], recv_sem=zr.at[step],
            device_id={"query": ((mz + step) % nz) * 2 + core}, device_id_type=MESH,
        )

    know_wait(2)
    for step in range(1, nz):
        z_copy(step).start()
    for step in range(1, nz):
        z_arrival(step).wait_recv()
    acc = zbuf[0].astype(F32)
    for step in range(1, nz):
        acc = acc + zbuf[step].astype(F32)
    fin[core] = acc
    fin_copy = pltpu.make_async_remote_copy(
        src_ref=fin.at[core], dst_ref=fin.at[core],
        send_sem=fs.at[0], recv_sem=fs.at[1], device_id=partner, device_id_type=MESH,
    )
    fin_copy.start()
    for slot in range(1, ROWS):
        query_copy(slot).wait_send()
        meta_copy(slot).wait_send()
        score_copy(slot).wait_send()
        grad_copy(slot).wait_send()
    for ix in range(SIDE):
        pair_copy(ix).wait_send()
    for step in range(1, nz):
        z_copy(step).wait_send()
    fin_arrival = pltpu.make_async_remote_copy(
        src_ref=fin.at[1 - core], dst_ref=fin.at[1 - core],
        send_sem=fs.at[0], recv_sem=fs.at[1], device_id=partner, device_id_type=MESH,
    )
    fin_arrival.wait_recv()
    fin_copy.wait_send()
    grad_ref[...] = fin[...].reshape(grad_ref.shape)


def hand_over(loss_in, grad_in, loss_ref, grad_ref):
    loss_ref[...] = loss_in[...]
    grad_ref[...] = grad_in[...]


def body(queries, hidden, proj, lists):
    qcount, qtok, width = queries.shape
    pcount, ptok, hwidth = hidden.shape
    nside = lax.axis_size("passage")
    nq = lax.axis_size("query")
    total = qcount * nq * nside
    share = hwidth // nside
    piece = ptok * pcount // PARTS
    block = qcount * qtok
    pairs = nside // 2
    nz = nq // 2
    dma = pltpu.SemaphoreType.DMA
    losses, grad = pl.pallas_call(
        functools.partial(kernel, total),
        out_shape=(
            jax.ShapeDtypeStruct((1, qcount), F32),
            jax.ShapeDtypeStruct((share, width), F32),
        ),
        in_specs=[pl.BlockSpec(memory_space=pl.ANY)] * 4,
        out_specs=(pl.BlockSpec(memory_space=pltpu.VMEM),) * 2,
        scratch_shapes=[
            pltpu.VMEM(queries.shape, BF16),
            pltpu.VMEM((ptok, pcount, hwidth), BF16),
            pltpu.VMEM(proj.shape, BF16),
            pltpu.VMEM(lists.shape, lists.dtype),
            pltpu.VMEM((nside * block, width), BF16),
            pltpu.VMEM((nside, 8, 128), BF16),
            pltpu.VMEM((128, 128), F32),
            pltpu.VMEM((128, 128), F32),
            pltpu.VMEM((PARTS, hwidth, piece), BF16),
            pltpu.VMEM((PARTS, piece, width), BF16),
            pltpu.VMEM((PARTS, piece, width), F32),
            pltpu.VMEM((PARTS, piece, width), F32),
            pltpu.VMEM((pairs, PARTS, piece, 2 * block), F32),
            pltpu.VMEM((pairs, 8, 2 * block), F32),
            pltpu.VMEM((pairs, 8, 2 * block), F32),
            pltpu.VMEM((nside, 8, 128), F32),
            pltpu.VMEM((pairs, 8, 2 * block), F32),
            pltpu.VMEM((PARTS, piece, width), BF16),
            pltpu.VMEM((nside, 2, share // 2, width), F32),
            pltpu.VMEM((nside, share // 2, width), BF16),
            pltpu.VMEM((nside, share // 2, width), BF16),
            pltpu.VMEM((nside, share // 2, width), F32),
            pltpu.VMEM((nside, share // 2, width), BF16),
            pltpu.VMEM((nside, share // 2, width), BF16),
            pltpu.VMEM((nz, share // 2, width), BF16),
            pltpu.VMEM((2, share // 2, width), F32),
            dma((4,)),
            dma((nside,)), dma((nside,)),
            dma((nside,)), dma((nside,)),
            dma((nside,)), dma((nside,)),
            dma((2, SIDE)),
            dma((nside,)), dma((nside,)),
            dma((nz,)), dma((nz,)),
            dma((2,)),
            pltpu.SemaphoreType.REGULAR((3, 2)),
        ],
        compiler_params=pltpu.CompilerParams(
            collective_id=0, has_side_effects=True, vmem_limit_bytes=60 * 1024 * 1024
        ),
        name="retriever_step",
    )(queries, hidden.transpose(1, 0, 2), proj, lists)
    losses, grad = pl.pallas_call(
        hand_over,
        out_shape=(
            jax.ShapeDtypeStruct((1, qcount), F32),
            jax.ShapeDtypeStruct((share, width), F32),
        ),
        in_specs=[pl.BlockSpec(memory_space=pltpu.VMEM)] * 2,
        out_specs=(pl.BlockSpec(memory_space=pltpu.VMEM),) * 2,
        name="outputs",
    )(losses, grad)
    return (losses.reshape(qcount), grad)


def solution(mesh):
    placed = (
        P(("query", "passage"), None, None),
        P(("query", "passage"), None, None),
        P(),
        P(("query", "passage"), None),
    )
    return jax.shard_map(
        body,
        mesh=mesh,
        in_specs=placed,
        out_specs=(P(("query", "passage")), P("passage", None)),
        check_vma=False,
    )
```

```python
import functools
import math

import jax
import jax.numpy as jnp
from jax import lax
from jax.experimental import pallas as pl
from jax.experimental.pallas import tpu as pltpu
from jax.sharding import PartitionSpec as P

BETA = 4.0
BETA2 = BETA * math.log2(math.e)
EPS = 1e-06
SIDE = 4
ROWS = SIDE * SIDE
F32 = jnp.float32
BF16 = jnp.bfloat16
NEGBIG = -3.0e38
PARTS = 3
MESH = pl.DeviceIdType.MESH


OFFSETS = (
    (0, 0),
    (1, 0), (-1, 0), (0, 1), (0, -1),
    (1, 1), (-1, -1), (1, -1), (-1, 1), (2, 0), (0, 2),
    (2, 1), (2, -1), (1, 2), (-1, 2),
    (2, 2),
)
X1, X3, Y1, Y3 = (1, 0), (-1, 0), (0, 1), (0, -1)
WAYS = {
    (1, 0): (X1,), (-1, 0): (X3,), (0, 1): (Y1,), (0, -1): (Y3,),
    (1, 1): (X1,), (-1, -1): (X3,), (1, -1): (Y3,), (-1, 1): (Y1,), (2, 0): (X1, X3), (0, 2): (Y1, Y3),
    (2, 1): (X1, X3), (2, -1): (X1, X3), (1, 2): (Y1, Y3), (-1, 2): (Y1, Y3),
    (2, 2): (X1, X3, Y1, Y3),
}


def wrapped(steps):
    return (steps + 1) % SIDE - 1


def make_hops():
    hops = []
    for offset in OFFSETS[1:]:
        for share, via in enumerate(WAYS[offset]):
            held = (wrapped(offset[0] - via[0]), wrapped(offset[1] - via[1]))
            hops.append((OFFSETS.index(offset), via, OFFSETS.index(held), share, len(WAYS[offset])))
    return tuple(hops)


HOPS = make_hops()
LINES = (2, -1, 1, 0)
STAGES = ((4, 0, 2), (10, 2, 5), (14, 5, 7), (15, 7, 8))


def spread(tile, lane, block):
    own = jnp.where(lane // 8 == block, tile, 0.0)
    for step in (8, 16, 32, 64):
        own = own + pltpu.roll(own, step, 1)
    return own


def kernel(
    total,
    queries_hbm, hidden_hbm, proj_hbm, lists_hbm,
    loss_ref, grad_ref,
    queries_ref, hidden_ref, proj_ref, lists_ref,
    qbuf, meta, mrows, mcols, turned, embed, unit, norm, expo, rsum, tops, score, scale, d_flat,
    part, given, precv, own, rsend, rrecv, zbuf, fin,
    ins, qs, qr, ms, mr, ss, sr, ps, rs, rr, zs, zr, fs, tok,
):
    qcount, qtok, width = queries_ref.shape
    ptok, pcount, hwidth = hidden_ref.shape
    nz = lax.axis_size("query") // 2
    qid = lax.axis_index("query")
    me = lax.axis_index("passage")
    mx, my = me // SIDE, me % SIDE
    mz, core = qid // 2, qid % 2
    partner = {"query": mz * 2 + (1 - core)}
    block = qcount * qtok
    half = grad_ref.shape[0] // 2
    piece = ptok * pcount // PARTS

    def along(step):
        return {"query": ((mz + nz + step) % nz) * 2 + core}

    loads = [
        pltpu.make_async_copy(src, dst, ins.at[n])
        for n, (src, dst) in enumerate(
            [(queries_hbm, queries_ref), (lists_hbm, lists_ref), (proj_hbm, proj_ref), (hidden_hbm, hidden_ref)]
        )
    ]

    def at_offset(dx, dy):
        return ((mx + SIDE + dx) % SIDE) * SIDE + (my + SIDE + dy) % SIDE

    def peer_of(slot):
        return at_offset(*OFFSETS[slot])

    def back_of(slot):
        dx, dy = OFFSETS[slot]
        return at_offset(-dx, -dy)

    barrier = pltpu.get_barrier_semaphore()
    for dx, dy in (X1, X3, Y1, Y3):
        pl.semaphore_signal(barrier, inc=1, device_id={"passage": at_offset(dx, dy)}, device_id_type=MESH)
    for step in (-1, 1):
        pl.semaphore_signal(barrier, inc=1, device_id=along(step), device_id_type=MESH)
    pl.semaphore_signal(barrier, inc=1, device_id=partner, device_id_type=MESH)
    for load in loads:
        load.start()

    def know_send(level):
        for side, step in enumerate((1, -1)):
            pl.semaphore_signal(
                tok.at[level, side], inc=1, device_id=along(step * (1 << level)), device_id_type=MESH
            )

    def know_wait(level):
        for side in range(2):
            pl.semaphore_wait(tok.at[level, side], 1)

    loads[0].wait()
    loads[1].wait()
    lane = lax.broadcasted_iota(jnp.int32, (8, 128), 1)
    row = lax.broadcasted_iota(jnp.int32, (block, block), 0)
    col = lax.broadcasted_iota(jnp.int32, (block, block), 1)
    order = jnp.where(col == (row % qcount) * qtok + row // qcount, 1.0, 0.0).astype(BF16)
    mine = jnp.dot(order, queries_ref[...].reshape(block, width), preferred_element_type=F32)
    qbuf[0:block, :] = mine.astype(BF16)

    listed = jnp.concatenate(
        [lists_ref[...].astype(F32), jnp.zeros((qcount, 128 - lists_ref.shape[1]), F32)], axis=1
    )
    listed = jnp.concatenate([listed, jnp.zeros((128 - qcount, 128), F32)], axis=0).T
    listed = listed[: lists_ref.shape[1], :]
    lrow = lax.broadcasted_iota(jnp.int32, (lists_ref.shape[1], 128), 1)
    number = jnp.where(lrow % 8 < pcount, (lrow // 8) * pcount + lrow % 8, -1).astype(F32)
    counts, firsts = [], []
    for query in range(qcount):
        hit = jnp.where(listed[:, query : query + 1] == number, 1.0, 0.0)
        counts.append(jnp.sum(hit, axis=0, keepdims=True))
        firsts.append(hit[0:1, :])
    tile = jnp.concatenate(counts + firsts, axis=0)
    meta[0] = tile.astype(BF16)

    pl.semaphore_wait(barrier, 4 + 2 + 1)
    know_send(0)

    def query_hop(number):
        slot, (dx, dy), held, share, shares = HOPS[number]
        rows = block // shares
        return pltpu.make_async_remote_copy(
            src_ref=qbuf.at[pl.ds(held * block + share * rows, rows)],
            dst_ref=qbuf.at[pl.ds(slot * block + share * rows, rows)],
            send_sem=qs.at[number], recv_sem=qr.at[number],
            device_id={"passage": at_offset(-dx, -dy)}, device_id_type=MESH,
        )

    def hand_on(slot):
        for number, hop in enumerate(HOPS):
            if hop[2] == slot:
                query_hop(number).start()

    def arrival(slot):
        for number, hop in enumerate(HOPS):
            if hop[0] == slot:
                query_hop(number).wait_recv()

    def meta_copy(slot):
        return pltpu.make_async_remote_copy(
            src_ref=meta.at[0], dst_ref=meta.at[slot],
            send_sem=ms.at[slot], recv_sem=mr.at[slot],
            device_id={"passage": back_of(slot)}, device_id_type=MESH,
        )

    def score_copy(slot):
        return pltpu.make_async_remote_copy(
            src_ref=score.at[0], dst_ref=score.at[slot],
            send_sem=ss.at[slot], recv_sem=sr.at[slot],
            device_id={"passage": back_of(slot)}, device_id_type=MESH,
        )

    hand_on(0)

    loads[2].wait()
    loads[3].wait()

    def project(chunk, carry):
        rows = pl.ds(chunk * (ptok // PARTS), ptok // PARTS)
        states = hidden_ref[rows].reshape(piece, hwidth)
        turned[chunk] = states.T
        flat = jnp.dot(states, proj_ref[...], preferred_element_type=F32)
        size = jnp.sqrt(jnp.sum(flat * flat, axis=1, keepdims=True) + EPS)
        one = flat / size
        norm[chunk] = jnp.broadcast_to(size, one.shape)
        unit[chunk] = one
        embed[chunk] = one.astype(BF16)
        return carry

    lax.fori_loop(0, PARTS, project, 0)
    know_wait(0)
    know_send(1)

    def score_pair(pair, carry):
        start = pl.multiple_of(pair * 2 * block, 2 * block)
        both = qbuf[pl.ds(start, 2 * block), :]
        top = None
        for chunk in range(PARTS):
            sims = lax.dot_general(
                embed[chunk], both, (((1,), (1,)), ((), ())), preferred_element_type=F32
            )
            expo[pair, chunk] = sims
            most = jnp.max(sims.reshape(piece // 8, 8, 2 * block), axis=0)
            top = most if top is None else jnp.maximum(top, most)
        top = jnp.maximum(top, pltpu.roll(top, 4, 0))
        mass = jnp.zeros_like(top)
        for chunk in range(PARTS):
            raised = jnp.exp2(BETA2 * (expo[pair, chunk].reshape(piece // 8, 8, 2 * block) - top[None]))
            expo[pair, chunk] = raised.reshape(piece, 2 * block)
            mass = mass + jnp.sum(raised, axis=0)
        mass = mass + pltpu.roll(mass, 4, 0)
        rsum[pair] = mass
        tops[pair] = top
        return carry

    arrived = 0
    for last, first_pair, end_pair in STAGES:
        for slot in range(arrived + 1, last + 1):
            arrival(slot)
            hand_on(slot)
        arrived = last
        if last == ROWS - 1:
            for slot in range(1, ROWS):
                meta_copy(slot).start()
        lax.fori_loop(first_pair, end_pair, score_pair, 0)
    found = jnp.zeros((8, 128), F32)
    for pair in range(ROWS // 2):
        lse = jnp.log(rsum[pair]) + BETA * tops[pair]
        for which in range(2):
            summed = lse[:, which * block : (which + 1) * block]
            for step in (4, 8, 16, 32, 64):
                summed = summed + pltpu.roll(summed, step, 1)
            found = jnp.where(lane // 8 == peer_of(2 * pair + which), summed, found)
    score[0] = found / BETA

    for slot in range(1, ROWS):
        score_copy(slot).start()

    know_wait(1)
    know_send(2)
    for slot in range(ROWS):
        if slot:
            meta_copy(slot).wait_recv()
        mrows[pl.ds(pl.multiple_of(8 * peer_of(slot), 8), 8), :] = meta[slot].astype(F32)
    mcols[...] = mrows[...].T

    top = jnp.full((8, 128), NEGBIG, F32)
    for slot in range(ROWS):
        if slot:
            score_copy(slot).wait_recv()
        count = mcols[pl.ds(pl.multiple_of(8 * peer_of(slot), 8), 8), :]
        top = jnp.maximum(top, jnp.where(count > 0, score[slot], NEGBIG))
    top = jnp.max(top, axis=0, keepdims=True)
    mass = jnp.zeros((8, 128), F32)
    shares = None
    for slot in range(ROWS):
        count = mcols[pl.ds(pl.multiple_of(8 * peer_of(slot), 8), 8), :]
        term = jnp.where(count > 0, count * jnp.exp(jnp.where(count > 0, score[slot], top) - top), 0.0)
        mass = mass + term
        if slot == 0:
            shares = term
    mass = jnp.sum(mass, axis=0, keepdims=True)
    top, mass = jnp.broadcast_to(top, (8, 128)), jnp.broadcast_to(mass, (8, 128))
    loss = jnp.log(mass) + top - pltpu.roll(top, 124, 1)
    loss = jnp.where(lane % 8 < 4, loss, pltpu.roll(loss, 4, 1))
    loss_ref[...] = spread(loss, lane, me)[0:1, :qcount]
    probs = shares / mass
    coef = (probs - pltpu.roll(probs, 124, 1)) / total
    coef = jnp.where(lane % 8 < 4, coef, pltpu.roll(coef, 4, 1))
    sub = lax.broadcasted_iota(jnp.int32, (8, 128), 0)
    coef = jnp.where(sub < 4, coef, pltpu.roll(coef, 4, 0))

    for pair in range(ROWS // 2):
        for which in range(2):
            wide = spread(coef, lane, peer_of(2 * pair + which))
            scale[pair, :, which * block : (which + 1) * block] = (
                wide / rsum[pair, :, which * block : (which + 1) * block]
            )

    def chunk_grad(chunk, carry):
        d_embed = None
        for pair in range(ROWS // 2):
            spreads = expo[pair, chunk].reshape(piece // 8, 8, 2 * block)
            weight = (spreads * scale[pair][None]).reshape(piece, 2 * block).astype(BF16)
            term = jnp.dot(
                weight, qbuf[pair * 2 * block : (pair + 1) * 2 * block, :], preferred_element_type=F32
            )
            d_embed = term if d_embed is None else d_embed + term
        one = unit[chunk]
        inner = jnp.sum(d_embed * one, axis=1, keepdims=True)
        d_flat[chunk] = ((d_embed - one * inner) / norm[chunk]).astype(BF16)
        return carry

    lax.fori_loop(0, PARTS, chunk_grad, 0)
    grown = None
    for chunk in range(PARTS):
        term = jnp.dot(turned[chunk], d_flat[chunk], preferred_element_type=F32)
        grown = term if grown is None else grown + term
    part[...] = grown.reshape(part.shape)
    given[...] = part[:, 1 - core].astype(BF16)

    def pair_copy(dx):
        line = pl.ds(((mx + SIDE - dx) % SIDE) * SIDE, SIDE)
        ix = LINES.index(dx)
        return pltpu.make_async_remote_copy(
            src_ref=given.at[line], dst_ref=precv.at[line],
            send_sem=ps.at[0, ix], recv_sem=ps.at[1, ix], device_id=partner, device_id_type=MESH,
        )

    for dx in LINES:
        pair_copy(dx).start()

    def grad_copy(slot):
        return pltpu.make_async_remote_copy(
            src_ref=rsend.at[back_of(slot)], dst_ref=rrecv.at[slot],
            send_sem=rs.at[slot], recv_sem=rr.at[slot],
            device_id={"passage": back_of(slot)}, device_id_type=MESH,
        )

    for dx in LINES:
        line = pl.ds(((mx + SIDE - dx) % SIDE) * SIDE, SIDE)
        pair_copy(dx).wait_recv()
        own[line] = part[line, core] + precv[line].astype(F32)
        rsend[line] = own[line].astype(BF16)
        for slot in range(ROWS - 1, 0, -1):
            if OFFSETS[slot][0] == dx:
                grad_copy(slot).start()
    acc = own[me]
    for slot in range(1, ROWS):
        grad_copy(slot).wait_recv()
        acc = acc + rrecv[slot].astype(F32)
    zbuf[mz] = acc.astype(BF16)

    def z_copy(step):
        return pltpu.make_async_remote_copy(
            src_ref=zbuf.at[mz], dst_ref=zbuf.at[mz],
            send_sem=zs.at[step], recv_sem=zr.at[step],
            device_id={"query": ((mz + step) % nz) * 2 + core}, device_id_type=MESH,
        )

    def z_arrival(step):
        source = (mz + nz - step) % nz
        return pltpu.make_async_remote_copy(
            src_ref=zbuf.at[source], dst_ref=zbuf.at[source],
            send_sem=zs.at[step], recv_sem=zr.at[step],
            device_id={"query": ((mz + step) % nz) * 2 + core}, device_id_type=MESH,
        )

    know_wait(2)
    for step in range(1, nz):
        z_copy(step).start()
    for step in range(1, nz):
        z_arrival(step).wait_recv()
    acc = zbuf[0].astype(F32)
    for step in range(1, nz):
        acc = acc + zbuf[step].astype(F32)
    fin[core] = acc
    fin_copy = pltpu.make_async_remote_copy(
        src_ref=fin.at[core], dst_ref=fin.at[core],
        send_sem=fs.at[0], recv_sem=fs.at[1], device_id=partner, device_id_type=MESH,
    )
    fin_copy.start()
    for number in range(len(HOPS)):
        query_hop(number).wait_send()
    for slot in range(1, ROWS):
        meta_copy(slot).wait_send()
        score_copy(slot).wait_send()
        grad_copy(slot).wait_send()
    for dx in LINES:
        pair_copy(dx).wait_send()
    for step in range(1, nz):
        z_copy(step).wait_send()
    fin_arrival = pltpu.make_async_remote_copy(
        src_ref=fin.at[1 - core], dst_ref=fin.at[1 - core],
        send_sem=fs.at[0], recv_sem=fs.at[1], device_id=partner, device_id_type=MESH,
    )
    fin_arrival.wait_recv()
    fin_copy.wait_send()
    grad_ref[...] = fin[...].reshape(grad_ref.shape)


def hand_over(loss_in, grad_in, loss_ref, grad_ref):
    loss_ref[...] = loss_in[...]
    grad_ref[...] = grad_in[...]


def body(queries, hidden, proj, lists):
    qcount, qtok, width = queries.shape
    pcount, ptok, hwidth = hidden.shape
    nside = lax.axis_size("passage")
    nq = lax.axis_size("query")
    total = qcount * nq * nside
    share = hwidth // nside
    piece = ptok * pcount // PARTS
    block = qcount * qtok
    pairs = nside // 2
    nz = nq // 2
    dma = pltpu.SemaphoreType.DMA
    losses, grad = pl.pallas_call(
        functools.partial(kernel, total),
        out_shape=(
            jax.ShapeDtypeStruct((1, qcount), F32),
            jax.ShapeDtypeStruct((share, width), F32),
        ),
        in_specs=[pl.BlockSpec(memory_space=pl.ANY)] * 4,
        out_specs=(pl.BlockSpec(memory_space=pltpu.VMEM),) * 2,
        scratch_shapes=[
            pltpu.VMEM(queries.shape, BF16),
            pltpu.VMEM((ptok, pcount, hwidth), BF16),
            pltpu.VMEM(proj.shape, BF16),
            pltpu.VMEM(lists.shape, lists.dtype),
            pltpu.VMEM((nside * block, width), BF16),
            pltpu.VMEM((nside, 8, 128), BF16),
            pltpu.VMEM((128, 128), F32),
            pltpu.VMEM((128, 128), F32),
            pltpu.VMEM((PARTS, hwidth, piece), BF16),
            pltpu.VMEM((PARTS, piece, width), BF16),
            pltpu.VMEM((PARTS, piece, width), F32),
            pltpu.VMEM((PARTS, piece, width), F32),
            pltpu.VMEM((pairs, PARTS, piece, 2 * block), F32),
            pltpu.VMEM((pairs, 8, 2 * block), F32),
            pltpu.VMEM((pairs, 8, 2 * block), F32),
            pltpu.VMEM((nside, 8, 128), F32),
            pltpu.VMEM((pairs, 8, 2 * block), F32),
            pltpu.VMEM((PARTS, piece, width), BF16),
            pltpu.VMEM((nside, 2, share // 2, width), F32),
            pltpu.VMEM((nside, share // 2, width), BF16),
            pltpu.VMEM((nside, share // 2, width), BF16),
            pltpu.VMEM((nside, share // 2, width), F32),
            pltpu.VMEM((nside, share // 2, width), BF16),
            pltpu.VMEM((nside, share // 2, width), BF16),
            pltpu.VMEM((nz, share // 2, width), BF16),
            pltpu.VMEM((2, share // 2, width), F32),
            dma((4,)),
            dma((len(HOPS),)), dma((len(HOPS),)),
            dma((nside,)), dma((nside,)),
            dma((nside,)), dma((nside,)),
            dma((2, SIDE)),
            dma((nside,)), dma((nside,)),
            dma((nz,)), dma((nz,)),
            dma((2,)),
            pltpu.SemaphoreType.REGULAR((3, 2)),
        ],
        compiler_params=pltpu.CompilerParams(
            collective_id=0, has_side_effects=True, vmem_limit_bytes=60 * 1024 * 1024
        ),
        name="retriever_step",
    )(queries, hidden.transpose(1, 0, 2), proj, lists)
    losses, grad = pl.pallas_call(
        hand_over,
        out_shape=(
            jax.ShapeDtypeStruct((1, qcount), F32),
            jax.ShapeDtypeStruct((share, width), F32),
        ),
        in_specs=[pl.BlockSpec(memory_space=pltpu.VMEM)] * 2,
        out_specs=(pl.BlockSpec(memory_space=pltpu.VMEM),) * 2,
        name="outputs",
    )(losses, grad)
    return (losses.reshape(qcount), grad)


def solution(mesh):
    placed = (
        P(("query", "passage"), None, None),
        P(("query", "passage"), None, None),
        P(),
        P(("query", "passage"), None),
    )
    return jax.shard_map(
        body,
        mesh=mesh,
        in_specs=placed,
        out_specs=(P(("query", "passage")), P("passage", None)),
        check_vma=False,
    )
```

```python
import functools
import math

import jax
import jax.numpy as jnp
from jax import lax
from jax.experimental import pallas as pl
from jax.experimental.pallas import tpu as pltpu
from jax.sharding import PartitionSpec as P

BETA = 4.0
BETA2 = BETA * math.log2(math.e)
EPS = 1e-06
SIDE = 4
ROWS = SIDE * SIDE
F32 = jnp.float32
BF16 = jnp.bfloat16
NEGBIG = -3.0e38
PARTS = 3
MESH = pl.DeviceIdType.MESH


def gray(index):
    return index ^ (index >> 1)


def spread(tile, lane, block):
    own = jnp.where(lane // 8 == block, tile, 0.0)
    for step in (8, 16, 32, 64):
        own = own + pltpu.roll(own, step, 1)
    return own


def kernel(
    total,
    queries_hbm, hidden_hbm, proj_hbm, lists_hbm,
    loss_ref, grad_ref,
    queries_ref, hidden_ref, proj_ref, lists_ref,
    qbuf, meta, mrows, mcols, turned, embed, unit, norm, expo, rsum, tops, score, scale, d_flat,
    part, given, precv, own, rsend, rrecv, zbuf, fin,
    ins, qs, qr, ms, mr, ss, sr, ps, rs, rr, zs, zr, fs, tok,
):
    qcount, qtok, width = queries_ref.shape
    ptok, pcount, hwidth = hidden_ref.shape
    nz = lax.axis_size("query") // 2
    qid = lax.axis_index("query")
    me = lax.axis_index("passage")
    mx, my = me // SIDE, me % SIDE
    mz, core = qid // 2, qid % 2
    partner = {"query": mz * 2 + (1 - core)}
    block = qcount * qtok
    half = grad_ref.shape[0] // 2
    piece = ptok * pcount // PARTS

    def along(step):
        return {"query": ((mz + nz + step) % nz) * 2 + core}

    loads = [
        pltpu.make_async_copy(src, dst, ins.at[n])
        for n, (src, dst) in enumerate(
            [(queries_hbm, queries_ref), (lists_hbm, lists_ref), (proj_hbm, proj_ref), (hidden_hbm, hidden_ref)]
        )
    ]

    def peer_of(slot):
        dx, dy = gray(slot // SIDE), gray(slot % SIDE)
        return ((mx + dx) % SIDE) * SIDE + (my + dy) % SIDE

    def back_of(slot):
        dx, dy = gray(slot // SIDE), gray(slot % SIDE)
        return ((mx + SIDE - dx) % SIDE) * SIDE + (my + SIDE - dy) % SIDE

    barrier = pltpu.get_barrier_semaphore()
    for slot in range(1, ROWS):
        pl.semaphore_signal(barrier, inc=1, device_id={"passage": peer_of(slot)}, device_id_type=MESH)

    for step in (-1, 1):
        pl.semaphore_signal(barrier, inc=1, device_id=along(step), device_id_type=MESH)
    pl.semaphore_signal(barrier, inc=1, device_id=partner, device_id_type=MESH)
    for load in loads:
        load.start()

    def know_send(level):
        for side, step in enumerate((1, -1)):
            pl.semaphore_signal(
                tok.at[level, side], inc=1, device_id=along(step * (1 << level)), device_id_type=MESH
            )

    def know_wait(level):
        for side in range(2):
            pl.semaphore_wait(tok.at[level, side], 1)

    loads[0].wait()
    loads[1].wait()
    lane = lax.broadcasted_iota(jnp.int32, (8, 128), 1)
    row = lax.broadcasted_iota(jnp.int32, (block, block), 0)
    col = lax.broadcasted_iota(jnp.int32, (block, block), 1)
    order = jnp.where(col == (row % qcount) * qtok + row // qcount, 1.0, 0.0).astype(BF16)
    mine = jnp.dot(order, queries_ref[...].reshape(block, width), preferred_element_type=F32)
    qbuf[0:block, :] = mine.astype(BF16)

    listed = jnp.concatenate(
        [lists_ref[...].astype(F32), jnp.zeros((qcount, 128 - lists_ref.shape[1]), F32)], axis=1
    )
    listed = jnp.concatenate([listed, jnp.zeros((128 - qcount, 128), F32)], axis=0).T
    listed = listed[: lists_ref.shape[1], :]
    lrow = lax.broadcasted_iota(jnp.int32, (lists_ref.shape[1], 128), 1)
    number = jnp.where(lrow % 8 < pcount, (lrow // 8) * pcount + lrow % 8, -1).astype(F32)
    counts, firsts = [], []
    for query in range(qcount):
        hit = jnp.where(listed[:, query : query + 1] == number, 1.0, 0.0)
        counts.append(jnp.sum(hit, axis=0, keepdims=True))
        firsts.append(hit[0:1, :])
    tile = jnp.concatenate(counts + firsts, axis=0)
    meta[0] = tile.astype(BF16)

    pl.semaphore_wait(barrier, ROWS - 1 + 2 + 1)
    know_send(0)

    def query_copy(slot):
        return pltpu.make_async_remote_copy(
            src_ref=qbuf.at[pl.ds(0, block)],
            dst_ref=qbuf.at[pl.ds(slot * block, block)],
            send_sem=qs.at[slot], recv_sem=qr.at[slot],
            device_id={"passage": back_of(slot)}, device_id_type=MESH,
        )

    def meta_copy(slot):
        return pltpu.make_async_remote_copy(
            src_ref=meta.at[0], dst_ref=meta.at[slot],
            send_sem=ms.at[slot], recv_sem=mr.at[slot],
            device_id={"passage": back_of(slot)}, device_id_type=MESH,
        )

    def score_copy(slot):
        return pltpu.make_async_remote_copy(
            src_ref=score.at[0], dst_ref=score.at[slot],
            send_sem=ss.at[slot], recv_sem=sr.at[slot],
            device_id={"passage": back_of(slot)}, device_id_type=MESH,
        )

    for slot in range(1, ROWS):
        query_copy(slot).start()
    for slot in range(1, ROWS):
        meta_copy(slot).start()

    loads[2].wait()
    loads[3].wait()

    def project(chunk, carry):
        rows = pl.ds(chunk * (ptok // PARTS), ptok // PARTS)
        states = hidden_ref[rows].reshape(piece, hwidth)
        turned[chunk] = states.T
        flat = jnp.dot(states, proj_ref[...], preferred_element_type=F32)
        size = jnp.sqrt(jnp.sum(flat * flat, axis=1, keepdims=True) + EPS)
        one = flat / size
        norm[chunk] = jnp.broadcast_to(size, one.shape)
        unit[chunk] = one
        embed[chunk] = one.astype(BF16)
        return carry

    lax.fori_loop(0, PARTS, project, 0)
    know_wait(0)
    know_send(1)

    def score_quad(quad, carry):
        @pl.when(quad > 0)
        def _():
            query_copy(4 * quad).wait_recv()

        for which in range(1, 4):
            query_copy(4 * quad + which).wait_recv()
        raw = []
        for which in range(2):
            start = pl.multiple_of((2 * quad + which) * 2 * block, 2 * block)
            both = qbuf[pl.ds(start, 2 * block), :]
            top, kept = None, []
            for chunk in range(PARTS):
                sims = lax.dot_general(
                    embed[chunk], both, (((1,), (1,)), ((), ())), preferred_element_type=F32
                ).reshape(piece // 8, 8, 2 * block)
                kept.append(sims)
                most = jnp.max(sims, axis=0)
                top = most if top is None else jnp.maximum(top, most)
            raw.append((kept, jnp.maximum(top, pltpu.roll(top, 4, 0))))
        for which in range(2):
            pair = 2 * quad + which
            kept, top = raw[which]
            mass = jnp.zeros_like(top)
            for chunk in range(PARTS):
                raised = jnp.exp2(BETA2 * (kept[chunk] - top[None]))
                expo[pair, chunk] = raised.reshape(piece, 2 * block)
                mass = mass + jnp.sum(raised, axis=0)
            rsum[pair] = mass + pltpu.roll(mass, 4, 0)
            tops[pair] = top
        return carry

    lax.fori_loop(0, ROWS // 4, score_quad, 0)
    found = jnp.zeros((8, 128), F32)
    for pair in range(ROWS // 2):
        lse = jnp.log(rsum[pair]) + BETA * tops[pair]
        for which in range(2):
            summed = lse[:, which * block : (which + 1) * block]
            for step in (4, 8, 16, 32, 64):
                summed = summed + pltpu.roll(summed, step, 1)
            found = jnp.where(lane // 8 == peer_of(2 * pair + which), summed, found)
    score[0] = found / BETA

    for slot in range(1, ROWS):
        score_copy(slot).start()

    know_wait(1)
    know_send(2)
    for slot in range(ROWS):
        if slot:
            meta_copy(slot).wait_recv()
        mrows[pl.ds(pl.multiple_of(8 * peer_of(slot), 8), 8), :] = meta[slot].astype(F32)
    mcols[...] = mrows[...].T

    top = jnp.full((8, 128), NEGBIG, F32)
    for slot in range(ROWS):
        if slot:
            score_copy(slot).wait_recv()
        count = mcols[pl.ds(pl.multiple_of(8 * peer_of(slot), 8), 8), :]
        top = jnp.maximum(top, jnp.where(count > 0, score[slot], NEGBIG))
    top = jnp.max(top, axis=0, keepdims=True)
    mass = jnp.zeros((8, 128), F32)
    shares = None
    for slot in range(ROWS):
        count = mcols[pl.ds(pl.multiple_of(8 * peer_of(slot), 8), 8), :]
        term = jnp.where(count > 0, count * jnp.exp(jnp.where(count > 0, score[slot], top) - top), 0.0)
        mass = mass + term
        if slot == 0:
            shares = term
    mass = jnp.sum(mass, axis=0, keepdims=True)
    top, mass = jnp.broadcast_to(top, (8, 128)), jnp.broadcast_to(mass, (8, 128))
    loss = jnp.log(mass) + top - pltpu.roll(top, 124, 1)
    loss = jnp.where(lane % 8 < 4, loss, pltpu.roll(loss, 4, 1))
    loss_ref[...] = spread(loss, lane, me)[0:1, :qcount]
    probs = shares / mass
    coef = (probs - pltpu.roll(probs, 124, 1)) / total
    coef = jnp.where(lane % 8 < 4, coef, pltpu.roll(coef, 4, 1))
    sub = lax.broadcasted_iota(jnp.int32, (8, 128), 0)
    coef = jnp.where(sub < 4, coef, pltpu.roll(coef, 4, 0))

    for pair in range(ROWS // 2):
        for which in range(2):
            wide = spread(coef, lane, peer_of(2 * pair + which))
            scale[pair, :, which * block : (which + 1) * block] = (
                wide / rsum[pair, :, which * block : (which + 1) * block]
            )

    def chunk_grad(chunk, carry):
        d_embed = None
        for pair in range(ROWS // 2):
            spreads = expo[pair, chunk].reshape(piece // 8, 8, 2 * block)
            weight = (spreads * scale[pair][None]).reshape(piece, 2 * block).astype(BF16)
            term = jnp.dot(
                weight, qbuf[pair * 2 * block : (pair + 1) * 2 * block, :], preferred_element_type=F32
            )
            d_embed = term if d_embed is None else d_embed + term
        one = unit[chunk]
        inner = jnp.sum(d_embed * one, axis=1, keepdims=True)
        d_flat[chunk] = ((d_embed - one * inner) / norm[chunk]).astype(BF16)
        return carry

    lax.fori_loop(0, PARTS, chunk_grad, 0)
    grown = None
    for chunk in range(PARTS):
        term = jnp.dot(turned[chunk], d_flat[chunk], preferred_element_type=F32)
        grown = term if grown is None else grown + term
    part[...] = grown.reshape(part.shape)
    given[...] = part[:, 1 - core].astype(BF16)

    def pair_copy(ix):
        line = pl.ds(((mx + SIDE - gray(ix)) % SIDE) * SIDE, SIDE)
        return pltpu.make_async_remote_copy(
            src_ref=given.at[line], dst_ref=precv.at[line],
            send_sem=ps.at[0, ix], recv_sem=ps.at[1, ix], device_id=partner, device_id_type=MESH,
        )

    for ix in (3, 2, 1, 0):
        pair_copy(ix).start()

    def grad_copy(slot):
        return pltpu.make_async_remote_copy(
            src_ref=rsend.at[back_of(slot)], dst_ref=rrecv.at[slot],
            send_sem=rs.at[slot], recv_sem=rr.at[slot],
            device_id={"passage": back_of(slot)}, device_id_type=MESH,
        )

    for ix in (3, 2, 1, 0):
        line = pl.ds(((mx + SIDE - gray(ix)) % SIDE) * SIDE, SIDE)
        pair_copy(ix).wait_recv()
        own[line] = part[line, core] + precv[line].astype(F32)
        rsend[line] = own[line].astype(BF16)
        for iy in (3, 2, 1, 0):
            if ix or iy:
                grad_copy(ix * SIDE + iy).start()
    acc = own[me]
    for slot in range(1, ROWS):
        grad_copy(slot).wait_recv()
        acc = acc + rrecv[slot].astype(F32)
    zbuf[mz] = acc.astype(BF16)

    def z_copy(step):
        return pltpu.make_async_remote_copy(
            src_ref=zbuf.at[mz], dst_ref=zbuf.at[mz],
            send_sem=zs.at[step], recv_sem=zr.at[step],
            device_id={"query": ((mz + step) % nz) * 2 + core}, device_id_type=MESH,
        )

    def z_arrival(step):
        source = (mz + nz - step) % nz
        return pltpu.make_async_remote_copy(
            src_ref=zbuf.at[source], dst_ref=zbuf.at[source],
            send_sem=zs.at[step], recv_sem=zr.at[step],
            device_id={"query": ((mz + step) % nz) * 2 + core}, device_id_type=MESH,
        )

    know_wait(2)
    for step in (8, 7, 9, 6, 10, 5, 11, 4, 12, 3, 13, 2, 14, 1, 15):
        z_copy(step).start()
    for step in range(1, nz):
        z_arrival(step).wait_recv()
    acc = zbuf[0].astype(F32)
    for step in range(1, nz):
        acc = acc + zbuf[step].astype(F32)
    fin[core] = acc
    fin_copy = pltpu.make_async_remote_copy(
        src_ref=fin.at[core], dst_ref=fin.at[core],
        send_sem=fs.at[0], recv_sem=fs.at[1], device_id=partner, device_id_type=MESH,
    )
    fin_copy.start()
    for slot in range(1, ROWS):
        query_copy(slot).wait_send()
        meta_copy(slot).wait_send()
        score_copy(slot).wait_send()
        grad_copy(slot).wait_send()
    for ix in range(SIDE):
        pair_copy(ix).wait_send()
    for step in range(1, nz):
        z_copy(step).wait_send()
    fin_arrival = pltpu.make_async_remote_copy(
        src_ref=fin.at[1 - core], dst_ref=fin.at[1 - core],
        send_sem=fs.at[0], recv_sem=fs.at[1], device_id=partner, device_id_type=MESH,
    )
    fin_arrival.wait_recv()
    fin_copy.wait_send()
    grad_ref[...] = fin[...].reshape(grad_ref.shape)


def hand_over(loss_in, grad_in, loss_ref, grad_ref):
    loss_ref[...] = loss_in[...]
    grad_ref[...] = grad_in[...]


def body(queries, hidden, proj, lists):
    qcount, qtok, width = queries.shape
    pcount, ptok, hwidth = hidden.shape
    nside = lax.axis_size("passage")
    nq = lax.axis_size("query")
    total = qcount * nq * nside
    share = hwidth // nside
    piece = ptok * pcount // PARTS
    block = qcount * qtok
    pairs = nside // 2
    nz = nq // 2
    dma = pltpu.SemaphoreType.DMA
    losses, grad = pl.pallas_call(
        functools.partial(kernel, total),
        out_shape=(
            jax.ShapeDtypeStruct((1, qcount), F32),
            jax.ShapeDtypeStruct((share, width), F32),
        ),
        in_specs=[pl.BlockSpec(memory_space=pl.ANY)] * 4,
        out_specs=(pl.BlockSpec(memory_space=pltpu.VMEM),) * 2,
        scratch_shapes=[
            pltpu.VMEM(queries.shape, BF16),
            pltpu.VMEM((ptok, pcount, hwidth), BF16),
            pltpu.VMEM(proj.shape, BF16),
            pltpu.VMEM(lists.shape, lists.dtype),
            pltpu.VMEM((nside * block, width), BF16),
            pltpu.VMEM((nside, 8, 128), BF16),
            pltpu.VMEM((128, 128), F32),
            pltpu.VMEM((128, 128), F32),
            pltpu.VMEM((PARTS, hwidth, piece), BF16),
            pltpu.VMEM((PARTS, piece, width), BF16),
            pltpu.VMEM((PARTS, piece, width), F32),
            pltpu.VMEM((PARTS, piece, width), F32),
            pltpu.VMEM((pairs, PARTS, piece, 2 * block), F32),
            pltpu.VMEM((pairs, 8, 2 * block), F32),
            pltpu.VMEM((pairs, 8, 2 * block), F32),
            pltpu.VMEM((nside, 8, 128), F32),
            pltpu.VMEM((pairs, 8, 2 * block), F32),
            pltpu.VMEM((PARTS, piece, width), BF16),
            pltpu.VMEM((nside, 2, share // 2, width), F32),
            pltpu.VMEM((nside, share // 2, width), BF16),
            pltpu.VMEM((nside, share // 2, width), BF16),
            pltpu.VMEM((nside, share // 2, width), F32),
            pltpu.VMEM((nside, share // 2, width), BF16),
            pltpu.VMEM((nside, share // 2, width), BF16),
            pltpu.VMEM((nz, share // 2, width), BF16),
            pltpu.VMEM((2, share // 2, width), F32),
            dma((4,)),
            dma((nside,)), dma((nside,)),
            dma((nside,)), dma((nside,)),
            dma((nside,)), dma((nside,)),
            dma((2, SIDE)),
            dma((nside,)), dma((nside,)),
            dma((nz,)), dma((nz,)),
            dma((2,)),
            pltpu.SemaphoreType.REGULAR((3, 2)),
        ],
        compiler_params=pltpu.CompilerParams(
            collective_id=0, has_side_effects=True, vmem_limit_bytes=60 * 1024 * 1024
        ),
        name="retriever_step",
    )(queries, hidden.transpose(1, 0, 2), proj, lists)
    losses, grad = pl.pallas_call(
        hand_over,
        out_shape=(
            jax.ShapeDtypeStruct((1, qcount), F32),
            jax.ShapeDtypeStruct((share, width), F32),
        ),
        in_specs=[pl.BlockSpec(memory_space=pltpu.VMEM)] * 2,
        out_specs=(pl.BlockSpec(memory_space=pltpu.VMEM),) * 2,
        name="outputs",
    )(losses, grad)
    return (losses.reshape(qcount), grad)


def solution(mesh):
    placed = (
        P(("query", "passage"), None, None),
        P(("query", "passage"), None, None),
        P(),
        P(("query", "passage"), None),
    )
    return jax.shard_map(
        body,
        mesh=mesh,
        in_specs=placed,
        out_specs=(P(("query", "passage")), P("passage", None)),
        check_vma=False,
    )
```

```python
import functools
import math

import jax
import jax.numpy as jnp
from jax import lax
from jax.experimental import pallas as pl
from jax.experimental.pallas import tpu as pltpu
from jax.sharding import PartitionSpec as P

BETA = 4.0
BETA2 = BETA * math.log2(math.e)
EPS = 1e-06
SIDE = 4
ROWS = SIDE * SIDE
F32 = jnp.float32
BF16 = jnp.bfloat16
NEGBIG = -3.0e38
PARTS = 3
MESH = pl.DeviceIdType.MESH


def gray(index):
    return index ^ (index >> 1)


def spread(tile, lane, block):
    own = jnp.where(lane // 8 == block, tile, 0.0)
    for step in (8, 16, 32, 64):
        own = own + pltpu.roll(own, step, 1)
    return own


def kernel(
    total,
    queries_hbm, hidden_hbm, proj_hbm, lists_hbm,
    loss_ref, grad_ref,
    queries_ref, hidden_ref, proj_ref, lists_ref,
    qbuf, meta, mrows, mcols, turned, embed, unit, norm, expo, rsum, tops, score, scale, d_flat,
    part, given, precv, own, rsend, rrecv, zbuf, fin,
    ins, qs, qr, ms, mr, ss, sr, ps, rs, rr, zs, zr, fs, tok,
):
    qcount, qtok, width = queries_ref.shape
    ptok, pcount, hwidth = hidden_ref.shape
    nz = lax.axis_size("query") // 2
    qid = lax.axis_index("query")
    me = lax.axis_index("passage")
    mx, my = me // SIDE, me % SIDE
    mz, core = qid // 2, qid % 2
    partner = {"query": mz * 2 + (1 - core)}
    block = qcount * qtok
    half = grad_ref.shape[0] // 2
    piece = ptok * pcount // PARTS

    def along(step):
        return {"query": ((mz + nz + step) % nz) * 2 + core}

    loads = [
        pltpu.make_async_copy(src, dst, ins.at[n])
        for n, (src, dst) in enumerate(
            [(queries_hbm, queries_ref), (lists_hbm, lists_ref), (proj_hbm, proj_ref), (hidden_hbm, hidden_ref)]
        )
    ]

    def peer_of(slot):
        dx, dy = gray(slot // SIDE), gray(slot % SIDE)
        return ((mx + dx) % SIDE) * SIDE + (my + dy) % SIDE

    def back_of(slot):
        dx, dy = gray(slot // SIDE), gray(slot % SIDE)
        return ((mx + SIDE - dx) % SIDE) * SIDE + (my + SIDE - dy) % SIDE

    barrier = pltpu.get_barrier_semaphore()
    for slot in range(1, ROWS):
        pl.semaphore_signal(barrier, inc=1, device_id={"passage": peer_of(slot)}, device_id_type=MESH)

    for step in (-1, 1):
        pl.semaphore_signal(barrier, inc=1, device_id=along(step), device_id_type=MESH)
    pl.semaphore_signal(barrier, inc=1, device_id=partner, device_id_type=MESH)
    for load in loads:
        load.start()

    def know_send(level):
        for side, step in enumerate((1, -1)):
            pl.semaphore_signal(
                tok.at[level, side], inc=1, device_id=along(step * (1 << level)), device_id_type=MESH
            )

    def know_wait(level):
        for side in range(2):
            pl.semaphore_wait(tok.at[level, side], 1)

    loads[0].wait()
    loads[1].wait()
    lane = lax.broadcasted_iota(jnp.int32, (8, 128), 1)
    row = lax.broadcasted_iota(jnp.int32, (block, block), 0)
    col = lax.broadcasted_iota(jnp.int32, (block, block), 1)
    order = jnp.where(col == (row % qcount) * qtok + row // qcount, 1.0, 0.0).astype(BF16)
    mine = jnp.dot(order, queries_ref[...].reshape(block, width), preferred_element_type=F32)
    qbuf[0:block, :] = mine.astype(BF16)

    listed = jnp.concatenate(
        [lists_ref[...].astype(F32), jnp.zeros((qcount, 128 - lists_ref.shape[1]), F32)], axis=1
    )
    listed = jnp.concatenate([listed, jnp.zeros((128 - qcount, 128), F32)], axis=0).T
    listed = listed[: lists_ref.shape[1], :]
    lrow = lax.broadcasted_iota(jnp.int32, (lists_ref.shape[1], 128), 1)
    number = jnp.where(lrow % 8 < pcount, (lrow // 8) * pcount + lrow % 8, -1).astype(F32)
    counts, firsts = [], []
    for query in range(qcount):
        hit = jnp.where(listed[:, query : query + 1] == number, 1.0, 0.0)
        counts.append(jnp.sum(hit, axis=0, keepdims=True))
        firsts.append(hit[0:1, :])
    tile = jnp.concatenate(counts + firsts, axis=0)
    meta[0] = tile.astype(BF16)

    pl.semaphore_wait(barrier, ROWS - 1 + 2 + 1)
    know_send(0)

    def query_copy(slot):
        return pltpu.make_async_remote_copy(
            src_ref=qbuf.at[pl.ds(0, block)],
            dst_ref=qbuf.at[pl.ds(slot * block, block)],
            send_sem=qs.at[slot], recv_sem=qr.at[slot],
            device_id={"passage": back_of(slot)}, device_id_type=MESH,
        )

    def meta_copy(slot):
        return pltpu.make_async_remote_copy(
            src_ref=meta.at[0], dst_ref=meta.at[slot],
            send_sem=ms.at[slot], recv_sem=mr.at[slot],
            device_id={"passage": back_of(slot)}, device_id_type=MESH,
        )

    def score_copy(slot):
        return pltpu.make_async_remote_copy(
            src_ref=score.at[0], dst_ref=score.at[slot],
            send_sem=ss.at[slot], recv_sem=sr.at[slot],
            device_id={"passage": back_of(slot)}, device_id_type=MESH,
        )

    for slot in range(1, ROWS):
        query_copy(slot).start()

    loads[2].wait()
    loads[3].wait()

    def project(chunk, carry):
        rows = pl.ds(chunk * (ptok // PARTS), ptok // PARTS)
        states = hidden_ref[rows].reshape(piece, hwidth)
        turned[chunk] = states.T
        flat = jnp.dot(states, proj_ref[...], preferred_element_type=F32)
        size = jnp.sqrt(jnp.sum(flat * flat, axis=1, keepdims=True) + EPS)
        one = flat / size
        norm[chunk] = jnp.broadcast_to(size, one.shape)
        unit[chunk] = one
        embed[chunk] = one.astype(BF16)
        return carry

    lax.fori_loop(0, PARTS, project, 0)
    know_wait(0)
    know_send(1)

    def score_quad(quad, carry):
        @pl.when(quad > 0)
        def _():
            query_copy(4 * quad).wait_recv()

        for which in range(1, 4):
            query_copy(4 * quad + which).wait_recv()
        raw = []
        for which in range(2):
            start = pl.multiple_of((2 * quad + which) * 2 * block, 2 * block)
            both = qbuf[pl.ds(start, 2 * block), :]
            top, kept = None, []
            for chunk in range(PARTS):
                sims = lax.dot_general(
                    embed[chunk], both, (((1,), (1,)), ((), ())), preferred_element_type=F32
                ).reshape(piece // 8, 8, 2 * block)
                kept.append(sims)
                most = jnp.max(sims, axis=0)
                top = most if top is None else jnp.maximum(top, most)
            raw.append((kept, jnp.maximum(top, pltpu.roll(top, 4, 0))))
        for which in range(2):
            pair = 2 * quad + which
            kept, top = raw[which]
            mass = jnp.zeros_like(top)
            for chunk in range(PARTS):
                raised = jnp.exp2(BETA2 * (kept[chunk] - top[None]))
                expo[pair, chunk] = raised.reshape(piece, 2 * block)
                mass = mass + jnp.sum(raised, axis=0)
            rsum[pair] = mass + pltpu.roll(mass, 4, 0)
            tops[pair] = top
        return carry

    lax.fori_loop(0, ROWS // 4, score_quad, 0)
    for slot in range(1, ROWS):
        meta_copy(slot).start()
    found = jnp.zeros((8, 128), F32)
    for pair in range(ROWS // 2):
        lse = jnp.log(rsum[pair]) + BETA * tops[pair]
        for which in range(2):
            summed = lse[:, which * block : (which + 1) * block]
            for step in (4, 8, 16, 32, 64):
                summed = summed + pltpu.roll(summed, step, 1)
            found = jnp.where(lane // 8 == peer_of(2 * pair + which), summed, found)
    score[0] = found / BETA

    for slot in range(1, ROWS):
        score_copy(slot).start()

    know_wait(1)
    know_send(2)
    for slot in range(ROWS):
        if slot:
            meta_copy(slot).wait_recv()
        mrows[pl.ds(pl.multiple_of(8 * peer_of(slot), 8), 8), :] = meta[slot].astype(F32)
    mcols[...] = mrows[...].T

    top = jnp.full((8, 128), NEGBIG, F32)
    for slot in range(ROWS):
        if slot:
            score_copy(slot).wait_recv()
        count = mcols[pl.ds(pl.multiple_of(8 * peer_of(slot), 8), 8), :]
        top = jnp.maximum(top, jnp.where(count > 0, score[slot], NEGBIG))
    top = jnp.max(top, axis=0, keepdims=True)
    mass = jnp.zeros((8, 128), F32)
    shares = None
    for slot in range(ROWS):
        count = mcols[pl.ds(pl.multiple_of(8 * peer_of(slot), 8), 8), :]
        term = jnp.where(count > 0, count * jnp.exp(jnp.where(count > 0, score[slot], top) - top), 0.0)
        mass = mass + term
        if slot == 0:
            shares = term
    mass = jnp.sum(mass, axis=0, keepdims=True)
    top, mass = jnp.broadcast_to(top, (8, 128)), jnp.broadcast_to(mass, (8, 128))
    loss = jnp.log(mass) + top - pltpu.roll(top, 124, 1)
    loss = jnp.where(lane % 8 < 4, loss, pltpu.roll(loss, 4, 1))
    loss_ref[...] = spread(loss, lane, me)[0:1, :qcount]
    probs = shares / mass
    coef = (probs - pltpu.roll(probs, 124, 1)) / total
    coef = jnp.where(lane % 8 < 4, coef, pltpu.roll(coef, 4, 1))
    sub = lax.broadcasted_iota(jnp.int32, (8, 128), 0)
    coef = jnp.where(sub < 4, coef, pltpu.roll(coef, 4, 0))

    for pair in range(ROWS // 2):
        for which in range(2):
            wide = spread(coef, lane, peer_of(2 * pair + which))
            scale[pair, :, which * block : (which + 1) * block] = (
                wide / rsum[pair, :, which * block : (which + 1) * block]
            )

    def chunk_grad(chunk, carry):
        d_embed = None
        for pair in range(ROWS // 2):
            spreads = expo[pair, chunk].reshape(piece // 8, 8, 2 * block)
            weight = (spreads * scale[pair][None]).reshape(piece, 2 * block).astype(BF16)
            term = jnp.dot(
                weight, qbuf[pair * 2 * block : (pair + 1) * 2 * block, :], preferred_element_type=F32
            )
            d_embed = term if d_embed is None else d_embed + term
        one = unit[chunk]
        inner = jnp.sum(d_embed * one, axis=1, keepdims=True)
        d_flat[chunk] = ((d_embed - one * inner) / norm[chunk]).astype(BF16)
        return carry

    lax.fori_loop(0, PARTS, chunk_grad, 0)
    grown = None
    for chunk in range(PARTS):
        term = jnp.dot(turned[chunk], d_flat[chunk], preferred_element_type=F32)
        grown = term if grown is None else grown + term
    part[...] = grown.reshape(part.shape)
    given[...] = part[:, 1 - core].astype(BF16)

    def pair_copy(ix):
        line = pl.ds(((mx + SIDE - gray(ix)) % SIDE) * SIDE, SIDE)
        return pltpu.make_async_remote_copy(
            src_ref=given.at[line], dst_ref=precv.at[line],
            send_sem=ps.at[0, ix], recv_sem=ps.at[1, ix], device_id=partner, device_id_type=MESH,
        )

    for ix in (3, 2, 1, 0):
        pair_copy(ix).start()

    def grad_copy(slot):
        return pltpu.make_async_remote_copy(
            src_ref=rsend.at[back_of(slot)], dst_ref=rrecv.at[slot],
            send_sem=rs.at[slot], recv_sem=rr.at[slot],
            device_id={"passage": back_of(slot)}, device_id_type=MESH,
        )

    for ix in (3, 2, 1, 0):
        line = pl.ds(((mx + SIDE - gray(ix)) % SIDE) * SIDE, SIDE)
        pair_copy(ix).wait_recv()
        own[line] = part[line, core] + precv[line].astype(F32)
        rsend[line] = own[line].astype(BF16)
        for iy in (3, 2, 1, 0):
            if ix or iy:
                grad_copy(ix * SIDE + iy).start()
    acc = own[me]
    for slot in range(1, ROWS):
        grad_copy(slot).wait_recv()
        acc = acc + rrecv[slot].astype(F32)
    zbuf[mz] = acc.astype(BF16)

    def z_copy(step):
        return pltpu.make_async_remote_copy(
            src_ref=zbuf.at[mz], dst_ref=zbuf.at[mz],
            send_sem=zs.at[step], recv_sem=zr.at[step],
            device_id={"query": ((mz + step) % nz) * 2 + core}, device_id_type=MESH,
        )

    def z_arrival(step):
        source = (mz + nz - step) % nz
        return pltpu.make_async_remote_copy(
            src_ref=zbuf.at[source], dst_ref=zbuf.at[source],
            send_sem=zs.at[step], recv_sem=zr.at[step],
            device_id={"query": ((mz + step) % nz) * 2 + core}, device_id_type=MESH,
        )

    know_wait(2)
    for step in (8, 7, 9, 6, 10, 5, 11, 4, 12, 3, 13, 2, 14, 1, 15):
        z_copy(step).start()
    for step in range(1, nz):
        z_arrival(step).wait_recv()
    acc = zbuf[0].astype(F32)
    for step in range(1, nz):
        acc = acc + zbuf[step].astype(F32)
    fin[core] = acc
    fin_copy = pltpu.make_async_remote_copy(
        src_ref=fin.at[core], dst_ref=fin.at[core],
        send_sem=fs.at[0], recv_sem=fs.at[1], device_id=partner, device_id_type=MESH,
    )
    fin_copy.start()
    for slot in range(1, ROWS):
        query_copy(slot).wait_send()
        meta_copy(slot).wait_send()
        score_copy(slot).wait_send()
        grad_copy(slot).wait_send()
    for ix in range(SIDE):
        pair_copy(ix).wait_send()
    for step in range(1, nz):
        z_copy(step).wait_send()
    fin_arrival = pltpu.make_async_remote_copy(
        src_ref=fin.at[1 - core], dst_ref=fin.at[1 - core],
        send_sem=fs.at[0], recv_sem=fs.at[1], device_id=partner, device_id_type=MESH,
    )
    fin_arrival.wait_recv()
    fin_copy.wait_send()
    grad_ref[...] = fin[...].reshape(grad_ref.shape)


def hand_over(loss_in, grad_in, loss_ref, grad_ref):
    loss_ref[...] = loss_in[...]
    grad_ref[...] = grad_in[...]


def body(queries, hidden, proj, lists):
    qcount, qtok, width = queries.shape
    pcount, ptok, hwidth = hidden.shape
    nside = lax.axis_size("passage")
    nq = lax.axis_size("query")
    total = qcount * nq * nside
    share = hwidth // nside
    piece = ptok * pcount // PARTS
    block = qcount * qtok
    pairs = nside // 2
    nz = nq // 2
    dma = pltpu.SemaphoreType.DMA
    losses, grad = pl.pallas_call(
        functools.partial(kernel, total),
        out_shape=(
            pltpu.VMEM((1, qcount), F32),
            pltpu.VMEM((share, width), F32),
        ),
        in_specs=[pl.BlockSpec(memory_space=pl.ANY)] * 4,
        out_specs=(pl.BlockSpec(memory_space=pltpu.VMEM),) * 2,
        scratch_shapes=[
            pltpu.VMEM(queries.shape, BF16),
            pltpu.VMEM((ptok, pcount, hwidth), BF16),
            pltpu.VMEM(proj.shape, BF16),
            pltpu.VMEM(lists.shape, lists.dtype),
            pltpu.VMEM((nside * block, width), BF16),
            pltpu.VMEM((nside, 8, 128), BF16),
            pltpu.VMEM((128, 128), F32),
            pltpu.VMEM((128, 128), F32),
            pltpu.VMEM((PARTS, hwidth, piece), BF16),
            pltpu.VMEM((PARTS, piece, width), BF16),
            pltpu.VMEM((PARTS, piece, width), F32),
            pltpu.VMEM((PARTS, piece, width), F32),
            pltpu.VMEM((pairs, PARTS, piece, 2 * block), F32),
            pltpu.VMEM((pairs, 8, 2 * block), F32),
            pltpu.VMEM((pairs, 8, 2 * block), F32),
            pltpu.VMEM((nside, 8, 128), F32),
            pltpu.VMEM((pairs, 8, 2 * block), F32),
            pltpu.VMEM((PARTS, piece, width), BF16),
            pltpu.VMEM((nside, 2, share // 2, width), F32),
            pltpu.VMEM((nside, share // 2, width), BF16),
            pltpu.VMEM((nside, share // 2, width), BF16),
            pltpu.VMEM((nside, share // 2, width), F32),
            pltpu.VMEM((nside, share // 2, width), BF16),
            pltpu.VMEM((nside, share // 2, width), BF16),
            pltpu.VMEM((nz, share // 2, width), BF16),
            pltpu.VMEM((2, share // 2, width), F32),
            dma((4,)),
            dma((nside,)), dma((nside,)),
            dma((nside,)), dma((nside,)),
            dma((nside,)), dma((nside,)),
            dma((2, SIDE)),
            dma((nside,)), dma((nside,)),
            dma((nz,)), dma((nz,)),
            dma((2,)),
            pltpu.SemaphoreType.REGULAR((3, 2)),
        ],
        compiler_params=pltpu.CompilerParams(
            collective_id=0, has_side_effects=True, vmem_limit_bytes=60 * 1024 * 1024
        ),
        name="retriever_step",
    )(queries, hidden.transpose(1, 0, 2), proj, lists)
    losses, grad = pl.pallas_call(
        hand_over,
        out_shape=(
            jax.ShapeDtypeStruct((1, qcount), F32),
            jax.ShapeDtypeStruct((share, width), F32),
        ),
        in_specs=[pl.BlockSpec(memory_space=pltpu.VMEM)] * 2,
        out_specs=(pl.BlockSpec(memory_space=pltpu.VMEM),) * 2,
        name="outputs",
    )(
        pltpu.with_memory_space_constraint(losses, pltpu.VMEM),
        pltpu.with_memory_space_constraint(grad, pltpu.VMEM),
    )
    return (losses.reshape(qcount), grad)


def solution(mesh):
    placed = (
        P(("query", "passage"), None, None),
        P(("query", "passage"), None, None),
        P(),
        P(("query", "passage"), None),
    )
    return jax.shard_map(
        body,
        mesh=mesh,
        in_specs=placed,
        out_specs=(P(("query", "passage")), P("passage", None)),
        check_vma=False,
    )
```

```python
import functools
import math

import jax
import jax.numpy as jnp
from jax import lax
from jax.experimental import pallas as pl
from jax.experimental.pallas import tpu as pltpu
from jax.sharding import PartitionSpec as P

BETA = 4.0
BETA2 = BETA * math.log2(math.e)
EPS = 1e-06
SIDE = 4
ROWS = SIDE * SIDE
F32 = jnp.float32
BF16 = jnp.bfloat16
NEGBIG = -3.0e38
PARTS = 3
MESH = pl.DeviceIdType.MESH


def gray(index):
    return index ^ (index >> 1)


def spread(tile, lane, block):
    own = jnp.where(lane // 8 == block, tile, 0.0)
    for step in (8, 16, 32, 64):
        own = own + pltpu.roll(own, step, 1)
    return own


def kernel(
    total,
    queries_hbm, hidden_hbm, proj_hbm, lists_hbm,
    loss_ref, grad_ref,
    queries_ref, hidden_ref, proj_ref, lists_ref,
    qbuf, meta, mrows, mcols, turned, embed, unit, norm, expo, rsum, tops, score, scale, d_flat,
    part, given, precv, own, rsend, rrecv, zbuf, fin,
    ins, qs, qr, ms, mr, ss, sr, ps, rs, rr, zs, zr, fs, tok,
):
    qcount, qtok, width = queries_ref.shape
    ptok, pcount, hwidth = hidden_ref.shape
    nz = lax.axis_size("query") // 2
    qid = lax.axis_index("query")
    me = lax.axis_index("passage")
    mx, my = me // SIDE, me % SIDE
    mz, core = qid // 2, qid % 2
    partner = {"query": mz * 2 + (1 - core)}
    block = qcount * qtok
    half = grad_ref.shape[0] // 2
    piece = ptok * pcount // PARTS

    def along(step):
        return {"query": ((mz + nz + step) % nz) * 2 + core}

    loads = [
        pltpu.make_async_copy(src, dst, ins.at[n])
        for n, (src, dst) in enumerate(
            [(queries_hbm, queries_ref), (lists_hbm, lists_ref), (proj_hbm, proj_ref), (hidden_hbm, hidden_ref)]
        )
    ]

    def peer_of(slot):
        dx, dy = gray(slot // SIDE), gray(slot % SIDE)
        return ((mx + dx) % SIDE) * SIDE + (my + dy) % SIDE

    def back_of(slot):
        dx, dy = gray(slot // SIDE), gray(slot % SIDE)
        return ((mx + SIDE - dx) % SIDE) * SIDE + (my + SIDE - dy) % SIDE

    barrier = pltpu.get_barrier_semaphore()
    for slot in range(1, ROWS):
        pl.semaphore_signal(barrier, inc=1, device_id={"passage": peer_of(slot)}, device_id_type=MESH)

    for step in (-1, 1):
        pl.semaphore_signal(barrier, inc=1, device_id=along(step), device_id_type=MESH)
    pl.semaphore_signal(barrier, inc=1, device_id=partner, device_id_type=MESH)
    for load in loads:
        load.start()

    def know_send(level):
        for side, step in enumerate((1, -1)):
            pl.semaphore_signal(
                tok.at[level, side], inc=1, device_id=along(step * (1 << level)), device_id_type=MESH
            )

    def know_wait(level):
        for side in range(2):
            pl.semaphore_wait(tok.at[level, side], 1)

    loads[0].wait()
    loads[1].wait()
    lane = lax.broadcasted_iota(jnp.int32, (8, 128), 1)
    row = lax.broadcasted_iota(jnp.int32, (block, block), 0)
    col = lax.broadcasted_iota(jnp.int32, (block, block), 1)
    order = jnp.where(col == (row % qcount) * qtok + row // qcount, 1.0, 0.0).astype(BF16)
    mine = jnp.dot(order, queries_ref[...].reshape(block, width), preferred_element_type=F32)
    qbuf[0:block, :] = mine.astype(BF16)

    listed = jnp.concatenate(
        [lists_ref[...].astype(F32), jnp.zeros((qcount, 128 - lists_ref.shape[1]), F32)], axis=1
    )
    listed = jnp.concatenate([listed, jnp.zeros((128 - qcount, 128), F32)], axis=0).T
    listed = listed[: lists_ref.shape[1], :]
    lrow = lax.broadcasted_iota(jnp.int32, (lists_ref.shape[1], 128), 1)
    number = jnp.where(lrow % 8 < pcount, (lrow // 8) * pcount + lrow % 8, -1).astype(F32)
    counts, firsts = [], []
    for query in range(qcount):
        hit = jnp.where(listed[:, query : query + 1] == number, 1.0, 0.0)
        counts.append(jnp.sum(hit, axis=0, keepdims=True))
        firsts.append(hit[0:1, :])
    tile = jnp.concatenate(counts + firsts, axis=0)
    meta[0] = tile.astype(BF16)

    pl.semaphore_wait(barrier, ROWS - 1 + 2 + 1)
    know_send(0)

    def query_copy(slot):
        return pltpu.make_async_remote_copy(
            src_ref=qbuf.at[pl.ds(0, block)],
            dst_ref=qbuf.at[pl.ds(slot * block, block)],
            send_sem=qs.at[slot], recv_sem=qr.at[slot],
            device_id={"passage": back_of(slot)}, device_id_type=MESH,
        )

    def meta_copy(slot):
        return pltpu.make_async_remote_copy(
            src_ref=meta.at[0], dst_ref=meta.at[slot],
            send_sem=ms.at[slot], recv_sem=mr.at[slot],
            device_id={"passage": back_of(slot)}, device_id_type=MESH,
        )

    def score_copy(slot):
        return pltpu.make_async_remote_copy(
            src_ref=score.at[0], dst_ref=score.at[slot],
            send_sem=ss.at[slot], recv_sem=sr.at[slot],
            device_id={"passage": back_of(slot)}, device_id_type=MESH,
        )

    for slot in range(1, ROWS):
        query_copy(slot).start()

    loads[2].wait()
    loads[3].wait()

    def project(chunk, carry):
        rows = pl.ds(chunk * (ptok // PARTS), ptok // PARTS)
        states = hidden_ref[rows].reshape(piece, hwidth)
        turned[chunk] = states.T
        flat = jnp.dot(states, proj_ref[...], preferred_element_type=F32)
        size = jnp.sqrt(jnp.sum(flat * flat, axis=1, keepdims=True) + EPS)
        one = flat / size
        norm[chunk] = jnp.broadcast_to(size, one.shape)
        unit[chunk] = one
        embed[chunk] = one.astype(BF16)
        return carry

    lax.fori_loop(0, PARTS, project, 0)
    know_wait(0)
    know_send(1)

    def score_quad(quad, carry):
        @pl.when(quad > 0)
        def _():
            query_copy(4 * quad).wait_recv()

        for which in range(1, 4):
            query_copy(4 * quad + which).wait_recv()
        raw = []
        for which in range(2):
            start = pl.multiple_of((2 * quad + which) * 2 * block, 2 * block)
            both = qbuf[pl.ds(start, 2 * block), :]
            top, kept = None, []
            for chunk in range(PARTS):
                sims = lax.dot_general(
                    embed[chunk], both, (((1,), (1,)), ((), ())), preferred_element_type=F32
                ).reshape(piece // 8, 8, 2 * block)
                kept.append(sims)
                most = jnp.max(sims, axis=0)
                top = most if top is None else jnp.maximum(top, most)
            raw.append((kept, jnp.maximum(top, pltpu.roll(top, 4, 0))))
        for which in range(2):
            pair = 2 * quad + which
            kept, top = raw[which]
            mass = jnp.zeros_like(top)
            for chunk in range(PARTS):
                raised = jnp.exp2(BETA2 * (kept[chunk] - top[None]))
                expo[pair, chunk] = raised.reshape(piece, 2 * block)
                mass = mass + jnp.sum(raised, axis=0)
            rsum[pair] = mass + pltpu.roll(mass, 4, 0)
            tops[pair] = top
        return carry

    lax.fori_loop(0, ROWS // 4, score_quad, 0)
    for slot in range(1, ROWS):
        meta_copy(slot).start()
    found = jnp.zeros((8, 128), F32)
    for pair in range(ROWS // 2):
        lse = jnp.log(rsum[pair]) + BETA * tops[pair]
        for which in range(2):
            summed = lse[:, which * block : (which + 1) * block]
            for step in (4, 8, 16, 32, 64):
                summed = summed + pltpu.roll(summed, step, 1)
            found = jnp.where(lane // 8 == peer_of(2 * pair + which), summed, found)
    score[0] = found / BETA

    for slot in range(1, ROWS):
        score_copy(slot).start()

    know_wait(1)
    know_send(2)
    for slot in range(ROWS):
        if slot:
            meta_copy(slot).wait_recv()
        mrows[pl.ds(pl.multiple_of(8 * peer_of(slot), 8), 8), :] = meta[slot].astype(F32)
    mcols[...] = mrows[...].T

    top = jnp.full((8, 128), NEGBIG, F32)
    for slot in range(ROWS):
        if slot:
            score_copy(slot).wait_recv()
        count = mcols[pl.ds(pl.multiple_of(8 * peer_of(slot), 8), 8), :]
        top = jnp.maximum(top, jnp.where(count > 0, score[slot], NEGBIG))
    top = jnp.max(top, axis=0, keepdims=True)
    mass = jnp.zeros((8, 128), F32)
    shares = None
    for slot in range(ROWS):
        count = mcols[pl.ds(pl.multiple_of(8 * peer_of(slot), 8), 8), :]
        term = jnp.where(count > 0, count * jnp.exp(jnp.where(count > 0, score[slot], top) - top), 0.0)
        mass = mass + term
        if slot == 0:
            shares = term
    mass = jnp.sum(mass, axis=0, keepdims=True)
    top, mass = jnp.broadcast_to(top, (8, 128)), jnp.broadcast_to(mass, (8, 128))
    loss = jnp.log(mass) + top - pltpu.roll(top, 124, 1)
    loss = jnp.where(lane % 8 < 4, loss, pltpu.roll(loss, 4, 1))
    loss_ref[...] = spread(loss, lane, me)[0:1, :qcount]
    probs = shares / mass
    coef = (probs - pltpu.roll(probs, 124, 1)) / total
    coef = jnp.where(lane % 8 < 4, coef, pltpu.roll(coef, 4, 1))
    sub = lax.broadcasted_iota(jnp.int32, (8, 128), 0)
    coef = jnp.where(sub < 4, coef, pltpu.roll(coef, 4, 0))

    for pair in range(ROWS // 2):
        for which in range(2):
            wide = spread(coef, lane, peer_of(2 * pair + which))
            scale[pair, :, which * block : (which + 1) * block] = (
                wide / rsum[pair, :, which * block : (which + 1) * block]
            )

    def chunk_grad(chunk, carry):
        d_embed = None
        for pair in range(ROWS // 2):
            spreads = expo[pair, chunk].reshape(piece // 8, 8, 2 * block)
            weight = (spreads * scale[pair][None]).reshape(piece, 2 * block).astype(BF16)
            term = jnp.dot(
                weight, qbuf[pair * 2 * block : (pair + 1) * 2 * block, :], preferred_element_type=F32
            )
            d_embed = term if d_embed is None else d_embed + term
        one = unit[chunk]
        inner = jnp.sum(d_embed * one, axis=1, keepdims=True)
        d_flat[chunk] = ((d_embed - one * inner) / norm[chunk]).astype(BF16)
        return carry

    for chunk in range(PARTS):
        chunk_grad(chunk, 0)
    grown = None
    for chunk in range(PARTS):
        term = jnp.dot(turned[chunk], d_flat[chunk], preferred_element_type=F32)
        grown = term if grown is None else grown + term
    part[...] = grown.reshape(part.shape)
    given[...] = part[:, 1 - core].astype(BF16)

    def pair_copy(ix):
        line = pl.ds(((mx + SIDE - gray(ix)) % SIDE) * SIDE, SIDE)
        return pltpu.make_async_remote_copy(
            src_ref=given.at[line], dst_ref=precv.at[line],
            send_sem=ps.at[0, ix], recv_sem=ps.at[1, ix], device_id=partner, device_id_type=MESH,
        )

    for ix in (3, 2, 1, 0):
        pair_copy(ix).start()

    def grad_copy(slot):
        return pltpu.make_async_remote_copy(
            src_ref=rsend.at[back_of(slot)], dst_ref=rrecv.at[slot],
            send_sem=rs.at[slot], recv_sem=rr.at[slot],
            device_id={"passage": back_of(slot)}, device_id_type=MESH,
        )

    for ix in (3, 2, 1, 0):
        line = pl.ds(((mx + SIDE - gray(ix)) % SIDE) * SIDE, SIDE)
        pair_copy(ix).wait_recv()
        own[line] = part[line, core] + precv[line].astype(F32)
        rsend[line] = own[line].astype(BF16)
        for iy in (3, 2, 1, 0):
            if ix or iy:
                grad_copy(ix * SIDE + iy).start()
    acc = own[me]
    for slot in range(1, ROWS):
        grad_copy(slot).wait_recv()
        acc = acc + rrecv[slot].astype(F32)
    zbuf[mz] = acc.astype(BF16)

    def z_copy(step):
        return pltpu.make_async_remote_copy(
            src_ref=zbuf.at[mz], dst_ref=zbuf.at[mz],
            send_sem=zs.at[step], recv_sem=zr.at[step],
            device_id={"query": ((mz + step) % nz) * 2 + core}, device_id_type=MESH,
        )

    def z_arrival(step):
        source = (mz + nz - step) % nz
        return pltpu.make_async_remote_copy(
            src_ref=zbuf.at[source], dst_ref=zbuf.at[source],
            send_sem=zs.at[step], recv_sem=zr.at[step],
            device_id={"query": ((mz + step) % nz) * 2 + core}, device_id_type=MESH,
        )

    know_wait(2)
    for step in (8, 7, 9, 6, 10, 5, 11, 4, 12, 3, 13, 2, 14, 1, 15):
        z_copy(step).start()
    for step in range(1, nz):
        z_arrival(step).wait_recv()
    acc = zbuf[0].astype(F32)
    for step in range(1, nz):
        acc = acc + zbuf[step].astype(F32)
    fin[core] = acc
    fin_copy = pltpu.make_async_remote_copy(
        src_ref=fin.at[core], dst_ref=fin.at[core],
        send_sem=fs.at[0], recv_sem=fs.at[1], device_id=partner, device_id_type=MESH,
    )
    fin_copy.start()
    for slot in range(1, ROWS):
        query_copy(slot).wait_send()
        meta_copy(slot).wait_send()
        score_copy(slot).wait_send()
        grad_copy(slot).wait_send()
    for ix in range(SIDE):
        pair_copy(ix).wait_send()
    for step in range(1, nz):
        z_copy(step).wait_send()
    fin_arrival = pltpu.make_async_remote_copy(
        src_ref=fin.at[1 - core], dst_ref=fin.at[1 - core],
        send_sem=fs.at[0], recv_sem=fs.at[1], device_id=partner, device_id_type=MESH,
    )
    fin_arrival.wait_recv()
    fin_copy.wait_send()
    grad_ref[...] = fin[...].reshape(grad_ref.shape)


def hand_over(loss_in, grad_in, loss_ref, grad_ref):
    loss_ref[...] = loss_in[...]
    grad_ref[...] = grad_in[...]


def body(queries, hidden, proj, lists):
    qcount, qtok, width = queries.shape
    pcount, ptok, hwidth = hidden.shape
    nside = lax.axis_size("passage")
    nq = lax.axis_size("query")
    total = qcount * nq * nside
    share = hwidth // nside
    piece = ptok * pcount // PARTS
    block = qcount * qtok
    pairs = nside // 2
    nz = nq // 2
    dma = pltpu.SemaphoreType.DMA
    losses, grad = pl.pallas_call(
        functools.partial(kernel, total),
        out_shape=(
            pltpu.VMEM((1, qcount), F32),
            pltpu.VMEM((share, width), F32),
        ),
        in_specs=[pl.BlockSpec(memory_space=pl.ANY)] * 4,
        out_specs=(pl.BlockSpec(memory_space=pltpu.VMEM),) * 2,
        scratch_shapes=[
            pltpu.VMEM(queries.shape, BF16),
            pltpu.VMEM((ptok, pcount, hwidth), BF16),
            pltpu.VMEM(proj.shape, BF16),
            pltpu.VMEM(lists.shape, lists.dtype),
            pltpu.VMEM((nside * block, width), BF16),
            pltpu.VMEM((nside, 8, 128), BF16),
            pltpu.VMEM((128, 128), F32),
            pltpu.VMEM((128, 128), F32),
            pltpu.VMEM((PARTS, hwidth, piece), BF16),
            pltpu.VMEM((PARTS, piece, width), BF16),
            pltpu.VMEM((PARTS, piece, width), F32),
            pltpu.VMEM((PARTS, piece, width), F32),
            pltpu.VMEM((pairs, PARTS, piece, 2 * block), F32),
            pltpu.VMEM((pairs, 8, 2 * block), F32),
            pltpu.VMEM((pairs, 8, 2 * block), F32),
            pltpu.VMEM((nside, 8, 128), F32),
            pltpu.VMEM((pairs, 8, 2 * block), F32),
            pltpu.VMEM((PARTS, piece, width), BF16),
            pltpu.VMEM((nside, 2, share // 2, width), F32),
            pltpu.VMEM((nside, share // 2, width), BF16),
            pltpu.VMEM((nside, share // 2, width), BF16),
            pltpu.VMEM((nside, share // 2, width), F32),
            pltpu.VMEM((nside, share // 2, width), BF16),
            pltpu.VMEM((nside, share // 2, width), BF16),
            pltpu.VMEM((nz, share // 2, width), BF16),
            pltpu.VMEM((2, share // 2, width), F32),
            dma((4,)),
            dma((nside,)), dma((nside,)),
            dma((nside,)), dma((nside,)),
            dma((nside,)), dma((nside,)),
            dma((2, SIDE)),
            dma((nside,)), dma((nside,)),
            dma((nz,)), dma((nz,)),
            dma((2,)),
            pltpu.SemaphoreType.REGULAR((3, 2)),
        ],
        compiler_params=pltpu.CompilerParams(
            collective_id=0, has_side_effects=True, vmem_limit_bytes=60 * 1024 * 1024
        ),
        name="retriever_step",
    )(queries, hidden.transpose(1, 0, 2), proj, lists)
    losses, grad = pl.pallas_call(
        hand_over,
        out_shape=(
            jax.ShapeDtypeStruct((1, qcount), F32),
            jax.ShapeDtypeStruct((share, width), F32),
        ),
        in_specs=[pl.BlockSpec(memory_space=pltpu.VMEM)] * 2,
        out_specs=(pl.BlockSpec(memory_space=pltpu.VMEM),) * 2,
        name="outputs",
    )(
        pltpu.with_memory_space_constraint(losses, pltpu.VMEM),
        pltpu.with_memory_space_constraint(grad, pltpu.VMEM),
    )
    return (losses.reshape(qcount), grad)


def solution(mesh):
    placed = (
        P(("query", "passage"), None, None),
        P(("query", "passage"), None, None),
        P(),
        P(("query", "passage"), None),
    )
    return jax.shard_map(
        body,
        mesh=mesh,
        in_specs=placed,
        out_specs=(P(("query", "passage")), P("passage", None)),
        check_vma=False,
    )
```

```python
import functools
import math

import jax
import jax.numpy as jnp
from jax import lax
from jax.experimental import pallas as pl
from jax.experimental.pallas import tpu as pltpu
from jax.sharding import PartitionSpec as P

BETA = 4.0
BETA2 = BETA * math.log2(math.e)
EPS = 1e-06
SIDE = 4
ROWS = SIDE * SIDE
F32 = jnp.float32
BF16 = jnp.bfloat16
NEGBIG = -3.0e38
PARTS = 3
MESH = pl.DeviceIdType.MESH


def gray(index):
    return index ^ (index >> 1)


def spread(tile, lane, block):
    own = jnp.where(lane // 8 == block, tile, 0.0)
    for step in (8, 16, 32, 64):
        own = own + pltpu.roll(own, step, 1)
    return own


def kernel(
    total,
    queries_hbm, hidden_hbm, proj_hbm, lists_hbm,
    loss_ref, grad_ref,
    queries_ref, hidden_ref, proj_ref, lists_ref,
    qbuf, meta, mrows, mcols, turned, embed, unit, norm, expo, rsum, tops, score, scale, d_flat,
    part, given, precv, own, rsend, rrecv, zbuf, fin,
    ins, qs, qr, ms, mr, ss, sr, ps, rs, rr, zs, zr, fs, tok,
):
    qcount, qtok, width = queries_ref.shape
    ptok, pcount, hwidth = hidden_ref.shape
    nz = lax.axis_size("query") // 2
    qid = lax.axis_index("query")
    me = lax.axis_index("passage")
    mx, my = me // SIDE, me % SIDE
    mz, core = qid // 2, qid % 2
    partner = {"query": mz * 2 + (1 - core)}
    block = qcount * qtok
    half = grad_ref.shape[0] // 2
    piece = ptok * pcount // PARTS

    def along(step):
        return {"query": ((mz + nz + step) % nz) * 2 + core}

    loads = [
        pltpu.make_async_copy(src, dst, ins.at[n])
        for n, (src, dst) in enumerate(
            [(queries_hbm, queries_ref), (lists_hbm, lists_ref), (proj_hbm, proj_ref), (hidden_hbm, hidden_ref)]
        )
    ]

    def peer_of(slot):
        dx, dy = gray(slot // SIDE), gray(slot % SIDE)
        return ((mx + dx) % SIDE) * SIDE + (my + dy) % SIDE

    def back_of(slot):
        dx, dy = gray(slot // SIDE), gray(slot % SIDE)
        return ((mx + SIDE - dx) % SIDE) * SIDE + (my + SIDE - dy) % SIDE

    barrier = pltpu.get_barrier_semaphore()
    for slot in range(1, ROWS):
        pl.semaphore_signal(barrier, inc=1, device_id={"passage": peer_of(slot)}, device_id_type=MESH)

    for step in (-1, 1):
        pl.semaphore_signal(barrier, inc=1, device_id=along(step), device_id_type=MESH)
    pl.semaphore_signal(barrier, inc=1, device_id=partner, device_id_type=MESH)
    for load in loads:
        load.start()

    def know_send(level):
        for side, step in enumerate((1, -1)):
            pl.semaphore_signal(
                tok.at[level, side], inc=1, device_id=along(step * (1 << level)), device_id_type=MESH
            )

    def know_wait(level):
        for side in range(2):
            pl.semaphore_wait(tok.at[level, side], 1)

    loads[0].wait()
    loads[1].wait()
    lane = lax.broadcasted_iota(jnp.int32, (8, 128), 1)
    row = lax.broadcasted_iota(jnp.int32, (block, block), 0)
    col = lax.broadcasted_iota(jnp.int32, (block, block), 1)
    order = jnp.where(col == (row % qcount) * qtok + row // qcount, 1.0, 0.0).astype(BF16)
    mine = jnp.dot(order, queries_ref[...].reshape(block, width), preferred_element_type=F32)
    qbuf[0:block, :] = mine.astype(BF16)

    listed = jnp.concatenate(
        [lists_ref[...].astype(F32), jnp.zeros((qcount, 128 - lists_ref.shape[1]), F32)], axis=1
    )
    listed = jnp.concatenate([listed, jnp.zeros((128 - qcount, 128), F32)], axis=0).T
    listed = listed[: lists_ref.shape[1], :]
    lrow = lax.broadcasted_iota(jnp.int32, (lists_ref.shape[1], 128), 1)
    number = jnp.where(lrow % 8 < pcount, (lrow // 8) * pcount + lrow % 8, -1).astype(F32)
    counts, firsts = [], []
    for query in range(qcount):
        hit = jnp.where(listed[:, query : query + 1] == number, 1.0, 0.0)
        counts.append(jnp.sum(hit, axis=0, keepdims=True))
        firsts.append(hit[0:1, :])
    tile = jnp.concatenate(counts + firsts, axis=0)
    meta[0] = tile.astype(BF16)

    pl.semaphore_wait(barrier, ROWS - 1 + 2 + 1)
    know_send(0)

    def query_copy(slot):
        return pltpu.make_async_remote_copy(
            src_ref=qbuf.at[pl.ds(0, block)],
            dst_ref=qbuf.at[pl.ds(slot * block, block)],
            send_sem=qs.at[slot], recv_sem=qr.at[slot],
            device_id={"passage": back_of(slot)}, device_id_type=MESH,
        )

    def meta_copy(slot):
        return pltpu.make_async_remote_copy(
            src_ref=meta.at[0], dst_ref=meta.at[slot],
            send_sem=ms.at[slot], recv_sem=mr.at[slot],
            device_id={"passage": back_of(slot)}, device_id_type=MESH,
        )

    def score_copy(slot):
        return pltpu.make_async_remote_copy(
            src_ref=score.at[0], dst_ref=score.at[slot],
            send_sem=ss.at[slot], recv_sem=sr.at[slot],
            device_id={"passage": back_of(slot)}, device_id_type=MESH,
        )

    for slot in range(1, ROWS):
        query_copy(slot).start()

    loads[2].wait()
    loads[3].wait()

    def project(chunk, carry):
        rows = pl.ds(chunk * (ptok // PARTS), ptok // PARTS)
        states = hidden_ref[rows].reshape(piece, hwidth)
        turned[chunk] = states.T
        flat = jnp.dot(states, proj_ref[...], preferred_element_type=F32)
        size = jnp.sqrt(jnp.sum(flat * flat, axis=1, keepdims=True) + EPS)
        one = flat / size
        norm[chunk] = jnp.broadcast_to(1.0 / size, one.shape)
        unit[chunk] = one
        embed[chunk] = one.astype(BF16)
        return carry

    lax.fori_loop(0, PARTS, project, 0)
    know_wait(0)
    know_send(1)

    def score_quad(quad, carry):
        @pl.when(quad > 0)
        def _():
            query_copy(4 * quad).wait_recv()

        for which in range(1, 4):
            query_copy(4 * quad + which).wait_recv()
        raw = []
        for which in range(2):
            start = pl.multiple_of((2 * quad + which) * 2 * block, 2 * block)
            both = qbuf[pl.ds(start, 2 * block), :]
            top, kept = None, []
            for chunk in range(PARTS):
                sims = lax.dot_general(
                    embed[chunk], both, (((1,), (1,)), ((), ())), preferred_element_type=F32
                ).reshape(piece // 8, 8, 2 * block)
                kept.append(sims)
                most = jnp.max(sims, axis=0)
                top = most if top is None else jnp.maximum(top, most)
            raw.append((kept, jnp.maximum(top, pltpu.roll(top, 4, 0))))
        for which in range(2):
            pair = 2 * quad + which
            kept, top = raw[which]
            mass = jnp.zeros_like(top)
            for chunk in range(PARTS):
                raised = jnp.exp2(BETA2 * (kept[chunk] - top[None]))
                expo[pair, chunk] = raised.reshape(piece, 2 * block)
                mass = mass + jnp.sum(raised, axis=0)
            rsum[pair] = mass + pltpu.roll(mass, 4, 0)
            tops[pair] = top
        return carry

    lax.fori_loop(0, ROWS // 4, score_quad, 0)
    for slot in range(1, ROWS):
        meta_copy(slot).start()
    found = jnp.zeros((8, 128), F32)
    for pair in range(ROWS // 2):
        lse = jnp.log(rsum[pair]) + BETA * tops[pair]
        for which in range(2):
            summed = lse[:, which * block : (which + 1) * block]
            for step in (4, 8, 16, 32, 64):
                summed = summed + pltpu.roll(summed, step, 1)
            found = jnp.where(lane // 8 == peer_of(2 * pair + which), summed, found)
    score[0] = found / BETA

    for slot in range(1, ROWS):
        score_copy(slot).start()

    know_wait(1)
    know_send(2)
    for slot in range(ROWS):
        if slot:
            meta_copy(slot).wait_recv()
        mrows[pl.ds(pl.multiple_of(8 * peer_of(slot), 8), 8), :] = meta[slot].astype(F32)
    mcols[...] = mrows[...].T

    top = jnp.full((8, 128), NEGBIG, F32)
    for slot in range(ROWS):
        if slot:
            score_copy(slot).wait_recv()
        count = mcols[pl.ds(pl.multiple_of(8 * peer_of(slot), 8), 8), :]
        top = jnp.maximum(top, jnp.where(count > 0, score[slot], NEGBIG))
    top = jnp.max(top, axis=0, keepdims=True)
    mass = jnp.zeros((8, 128), F32)
    shares = None
    for slot in range(ROWS):
        count = mcols[pl.ds(pl.multiple_of(8 * peer_of(slot), 8), 8), :]
        term = jnp.where(count > 0, count * jnp.exp(jnp.where(count > 0, score[slot], top) - top), 0.0)
        mass = mass + term
        if slot == 0:
            shares = term
    mass = jnp.sum(mass, axis=0, keepdims=True)
    top, mass = jnp.broadcast_to(top, (8, 128)), jnp.broadcast_to(mass, (8, 128))
    loss = jnp.log(mass) + top - pltpu.roll(top, 124, 1)
    loss = jnp.where(lane % 8 < 4, loss, pltpu.roll(loss, 4, 1))
    loss_ref[...] = spread(loss, lane, me)[0:1, :qcount]
    probs = shares / mass
    coef = (probs - pltpu.roll(probs, 124, 1)) / total
    coef = jnp.where(lane % 8 < 4, coef, pltpu.roll(coef, 4, 1))
    sub = lax.broadcasted_iota(jnp.int32, (8, 128), 0)
    coef = jnp.where(sub < 4, coef, pltpu.roll(coef, 4, 0))

    for pair in range(ROWS // 2):
        for which in range(2):
            wide = spread(coef, lane, peer_of(2 * pair + which))
            scale[pair, :, which * block : (which + 1) * block] = (
                wide / rsum[pair, :, which * block : (which + 1) * block]
            )

    def chunk_grad(chunk, carry):
        d_embed = None
        for pair in range(ROWS // 2):
            spreads = expo[pair, chunk].reshape(piece // 8, 8, 2 * block)
            weight = (spreads * scale[pair][None]).reshape(piece, 2 * block).astype(BF16)
            term = jnp.dot(
                weight, qbuf[pair * 2 * block : (pair + 1) * 2 * block, :], preferred_element_type=F32
            )
            d_embed = term if d_embed is None else d_embed + term
        one = unit[chunk]
        inner = jnp.sum(d_embed * one, axis=1, keepdims=True)
        d_flat[chunk] = ((d_embed - one * inner) * norm[chunk]).astype(BF16)
        return carry

    for chunk in range(PARTS):
        chunk_grad(chunk, 0)
    grown = None
    for chunk in range(PARTS):
        term = jnp.dot(turned[chunk], d_flat[chunk], preferred_element_type=F32)
        grown = term if grown is None else grown + term
    part[...] = grown.reshape(part.shape)
    given[...] = part[:, 1 - core].astype(BF16)

    def pair_copy(ix):
        line = pl.ds(((mx + SIDE - gray(ix)) % SIDE) * SIDE, SIDE)
        return pltpu.make_async_remote_copy(
            src_ref=given.at[line], dst_ref=precv.at[line],
            send_sem=ps.at[0, ix], recv_sem=ps.at[1, ix], device_id=partner, device_id_type=MESH,
        )

    for ix in (3, 2, 1, 0):
        pair_copy(ix).start()

    def grad_copy(slot):
        return pltpu.make_async_remote_copy(
            src_ref=rsend.at[back_of(slot)], dst_ref=rrecv.at[slot],
            send_sem=rs.at[slot], recv_sem=rr.at[slot],
            device_id={"passage": back_of(slot)}, device_id_type=MESH,
        )

    for ix in (3, 2, 1, 0):
        line = pl.ds(((mx + SIDE - gray(ix)) % SIDE) * SIDE, SIDE)
        pair_copy(ix).wait_recv()
        own[line] = part[line, core] + precv[line].astype(F32)
        rsend[line] = own[line].astype(BF16)
        for iy in (3, 2, 1, 0):
            if ix or iy:
                grad_copy(ix * SIDE + iy).start()
    acc = own[me]
    for slot in range(1, ROWS):
        grad_copy(slot).wait_recv()
        acc = acc + rrecv[slot].astype(F32)
    zbuf[mz] = acc.astype(BF16)

    def z_copy(step):
        return pltpu.make_async_remote_copy(
            src_ref=zbuf.at[mz], dst_ref=zbuf.at[mz],
            send_sem=zs.at[step], recv_sem=zr.at[step],
            device_id={"query": ((mz + step) % nz) * 2 + core}, device_id_type=MESH,
        )

    def z_arrival(step):
        source = (mz + nz - step) % nz
        return pltpu.make_async_remote_copy(
            src_ref=zbuf.at[source], dst_ref=zbuf.at[source],
            send_sem=zs.at[step], recv_sem=zr.at[step],
            device_id={"query": ((mz + step) % nz) * 2 + core}, device_id_type=MESH,
        )

    know_wait(2)
    for step in (8, 7, 9, 6, 10, 5, 11, 4, 12, 3, 13, 2, 14, 1, 15):
        z_copy(step).start()
    for step in range(1, nz):
        z_arrival(step).wait_recv()
    acc = zbuf[0].astype(F32)
    for step in range(1, nz):
        acc = acc + zbuf[step].astype(F32)
    fin[core] = acc
    fin_copy = pltpu.make_async_remote_copy(
        src_ref=fin.at[core], dst_ref=fin.at[core],
        send_sem=fs.at[0], recv_sem=fs.at[1], device_id=partner, device_id_type=MESH,
    )
    fin_copy.start()
    for slot in range(1, ROWS):
        query_copy(slot).wait_send()
        meta_copy(slot).wait_send()
        score_copy(slot).wait_send()
        grad_copy(slot).wait_send()
    for ix in range(SIDE):
        pair_copy(ix).wait_send()
    for step in range(1, nz):
        z_copy(step).wait_send()
    fin_arrival = pltpu.make_async_remote_copy(
        src_ref=fin.at[1 - core], dst_ref=fin.at[1 - core],
        send_sem=fs.at[0], recv_sem=fs.at[1], device_id=partner, device_id_type=MESH,
    )
    fin_arrival.wait_recv()
    fin_copy.wait_send()
    grad_ref[...] = fin[...].reshape(grad_ref.shape)


def hand_over(loss_in, grad_in, loss_ref, grad_ref):
    loss_ref[...] = loss_in[...]
    grad_ref[...] = grad_in[...]


def body(queries, hidden, proj, lists):
    qcount, qtok, width = queries.shape
    pcount, ptok, hwidth = hidden.shape
    nside = lax.axis_size("passage")
    nq = lax.axis_size("query")
    total = qcount * nq * nside
    share = hwidth // nside
    piece = ptok * pcount // PARTS
    block = qcount * qtok
    pairs = nside // 2
    nz = nq // 2
    dma = pltpu.SemaphoreType.DMA
    losses, grad = pl.pallas_call(
        functools.partial(kernel, total),
        out_shape=(
            pltpu.VMEM((1, qcount), F32),
            pltpu.VMEM((share, width), F32),
        ),
        in_specs=[pl.BlockSpec(memory_space=pl.ANY)] * 4,
        out_specs=(pl.BlockSpec(memory_space=pltpu.VMEM),) * 2,
        scratch_shapes=[
            pltpu.VMEM(queries.shape, BF16),
            pltpu.VMEM((ptok, pcount, hwidth), BF16),
            pltpu.VMEM(proj.shape, BF16),
            pltpu.VMEM(lists.shape, lists.dtype),
            pltpu.VMEM((nside * block, width), BF16),
            pltpu.VMEM((nside, 8, 128), BF16),
            pltpu.VMEM((128, 128), F32),
            pltpu.VMEM((128, 128), F32),
            pltpu.VMEM((PARTS, hwidth, piece), BF16),
            pltpu.VMEM((PARTS, piece, width), BF16),
            pltpu.VMEM((PARTS, piece, width), F32),
            pltpu.VMEM((PARTS, piece, width), F32),
            pltpu.VMEM((pairs, PARTS, piece, 2 * block), F32),
            pltpu.VMEM((pairs, 8, 2 * block), F32),
            pltpu.VMEM((pairs, 8, 2 * block), F32),
            pltpu.VMEM((nside, 8, 128), F32),
            pltpu.VMEM((pairs, 8, 2 * block), F32),
            pltpu.VMEM((PARTS, piece, width), BF16),
            pltpu.VMEM((nside, 2, share // 2, width), F32),
            pltpu.VMEM((nside, share // 2, width), BF16),
            pltpu.VMEM((nside, share // 2, width), BF16),
            pltpu.VMEM((nside, share // 2, width), F32),
            pltpu.VMEM((nside, share // 2, width), BF16),
            pltpu.VMEM((nside, share // 2, width), BF16),
            pltpu.VMEM((nz, share // 2, width), BF16),
            pltpu.VMEM((2, share // 2, width), F32),
            dma((4,)),
            dma((nside,)), dma((nside,)),
            dma((nside,)), dma((nside,)),
            dma((nside,)), dma((nside,)),
            dma((2, SIDE)),
            dma((nside,)), dma((nside,)),
            dma((nz,)), dma((nz,)),
            dma((2,)),
            pltpu.SemaphoreType.REGULAR((3, 2)),
        ],
        compiler_params=pltpu.CompilerParams(
            collective_id=0, has_side_effects=True, vmem_limit_bytes=60 * 1024 * 1024
        ),
        name="retriever_step",
    )(queries, hidden.transpose(1, 0, 2), proj, lists)
    losses, grad = pl.pallas_call(
        hand_over,
        out_shape=(
            jax.ShapeDtypeStruct((1, qcount), F32),
            jax.ShapeDtypeStruct((share, width), F32),
        ),
        in_specs=[pl.BlockSpec(memory_space=pltpu.VMEM)] * 2,
        out_specs=(pl.BlockSpec(memory_space=pltpu.VMEM),) * 2,
        name="outputs",
    )(
        pltpu.with_memory_space_constraint(losses, pltpu.VMEM),
        pltpu.with_memory_space_constraint(grad, pltpu.VMEM),
    )
    return (losses.reshape(qcount), grad)


def solution(mesh):
    placed = (
        P(("query", "passage"), None, None),
        P(("query", "passage"), None, None),
        P(),
        P(("query", "passage"), None),
    )
    return jax.shard_map(
        body,
        mesh=mesh,
        in_specs=placed,
        out_specs=(P(("query", "passage")), P("passage", None)),
        check_vma=False,
    )
```
